32 devices in a mesh: group: 2 (over y), space: 4 (over x, core), src: 4 (over z).
Axes of the slice: x: 2, y: 2, z: 4, core: 2. Of those that a mesh axis runs over, the one named last changes fastest.
Arguments:
- conductivity: float32 [128, 32, 128], P(('group', 'space')), parts along dimension 0, may hold values from 0.2 to 5
- prior_potential: float32 [8, 64, 32, 128], P(('group', 'src'), 'space'), parts along dimension 0, may hold values from -6 to 6
- electrodes: int32 [8, 2], P(('group', 'src')), parts along dimension 0, may hold values from 0 to 262143
- currents: float32 [8], P(('group', 'src')), parts along dimension 0, may hold values from 2 to 20
- receivers: int32 [512], P('group'), parts along dimension 0, may hold values from 0 to 262143
- observed: float32 [8, 256], P(('group', 'src')), parts along dimension 0, may hold values from -3 to 3
Outputs:
- potential: float32 [8, 64, 32, 128], P(('group', 'src'), 'space'), parts along dimension 0
- misfit: float32 [8, 256], P(('group', 'src')), parts along dimension 0
- gradient: float32 [128, 32, 128], P(('group', 'space')), parts along dimension 0
The draws below stay inside these ranges and needn't reach their ends.
There are 2 independent parts, one for each index of `group`. The reference program is written for one: setup_inputs(seed, part) draws one part's arguments, and reference() takes and returns one part's arrays. A program takes and returns all parts, laid end to end along the dimension named above; each array names one. Nothing has to cross between parts.
Inputs may be any that keep to these rules, and one draw needn't show every extreme that they name: Flat cell indices x * 32 * 128 + y * 128 + z; a source's two electrodes may fall in any cells. Flat cell indices as for electrodes; two receivers may share a cell.
All inputs are finite; a program needn't handle non-finite values.
Results may differ from the reference program's by a relative error of at most 0.0003.
Values sent between devices are 32-bit elements; how exact they have to be, the bound alone decides.
No kernel may reach another device: no remote copies, remote signals or barrier semaphores. Data moves between devices by JAX's collectives and lax.ppermute only.
A program may use at most 128 MiB of HBM per device.

```python
import math
import jax
import jax.numpy as jnp
from jax import lax

NY = 32
NZ = 128
NREC = 256
LEVELS = 4
COARSE_SWEEPS = 4
NX = 64
NSRC = 4
NCELLS = 262144


def touch_ends(values, key, low, high):
    dims = values.shape
    index_at = [jax.random.randint(jax.random.fold_in(key, axis), (), 0, dims[axis]) for axis in range(len(dims))]
    values = values.at[tuple(index_at)].set(low)
    longest = dims.index(max(dims))
    index_at[longest] = (index_at[longest] + 1) % dims[longest]
    return values.at[tuple(index_at)].set(high)


def shard_levels(stream_key, shape, split, least, top_value):
    gain = 1.0
    for position, blocks in split:
        heights = jax.random.uniform(jax.random.fold_in(jax.random.fold_in(stream_key, 6), position), (blocks,), jnp.float32, least / len(split), top_value / len(split))
        gain = gain * jnp.repeat(jnp.exp(heights), shape[position] // blocks).reshape((-1,) + (1,) * (len(shape) - 1 - position))
    return gain


def centred(stream_key, dims, spread, most, split=(), kind=jnp.bfloat16):
    result = jax.random.normal(stream_key, dims, jnp.float32) * spread
    if len(split) > 0:
        result = shard_levels(stream_key, dims, split, -0.22, 0.18) * result
    return jnp.clip(result, min=-most, max=most).astype(kind)


def setup_inputs(seed: int = 0, part: int = 0) -> dict:
    streams_of = jax.random.split(jax.random.key(seed), 7)
    part_splits = jax.random.split(jax.random.fold_in(streams_of[6], part), 7)
    return {
        "conductivity": jnp.clip(jnp.exp(math.log(5.0) - 3.218876 * jax.random.uniform(part_splits[0], (NX, NY, NZ), jnp.float32) ** shard_levels(part_splits[0], (NX, NY, NZ), ((0, 4),), -0.2, 0.2)), 0.2, 5.0),
        "prior_potential": centred(part_splits[1], (NSRC, NX, NY, NZ), 1.0, 6.0, ((0, 4), (1, 4)), jnp.float32),
        "electrodes": touch_ends(jax.random.randint(part_splits[2], (NSRC, 2), 0, NCELLS), jax.random.fold_in(part_splits[2], 1), 0, NCELLS - 1).astype(jnp.int32),
        "currents": jnp.clip(jnp.exp(math.log(20.0) - 2.3025851 * jax.random.uniform(part_splits[3], (NSRC,), jnp.float32) ** shard_levels(part_splits[3], (NSRC,), ((0, 4),), -0.2, 0.2)), 2.0, 20.0),
        "receivers": touch_ends(jax.random.randint(part_splits[4], (NREC,), 0, NCELLS), jax.random.fold_in(part_splits[4], 1), 0, NCELLS - 1).astype(jnp.int32),
        "observed": centred(part_splits[5], (NSRC, NREC), 0.5, 3.0, ((0, 4),), jnp.float32),
    }


OFFSETS = ((1, 0, 0), (-1, 0, 0), (0, 1, 0), (0, -1, 0), (0, 0, 1), (0, 0, -1))


def shifted(array, step):
    size_x, size_y, size_z = array.shape[-3:]
    return array[..., 1 + step[0]:size_x - 1 + step[0], 1 + step[1]:size_y - 1 + step[1], 1 + step[2]:size_z - 1 + step[2]]


def couplings(sigma_ext, weight):
    padded = jnp.pad(sigma_ext, ((0, 0), (1, 1), (1, 1)))
    centre = shifted(padded, (0, 0, 0))
    return [weight * 0.5 * (centre + shifted(padded, step)) for step in OFFSETS]


def diagonal_of(coupled):
    summed = coupled[0]
    for coupling in coupled[1:]:
        summed = summed + coupling
    return summed


def neighbours(field_ext, coupled):
    padded = jnp.pad(field_ext, ((0, 0), (0, 0), (1, 1), (1, 1)))
    summed = coupled[0] * shifted(padded, OFFSETS[0])
    for coupling, step in zip(coupled[1:], OFFSETS[1:]):
        summed = summed + coupling * shifted(padded, step)
    return summed


def relax(field_ext, right_side, coupled, diagonal, colour_mask):
    update = (right_side + neighbours(field_ext, coupled)) / diagonal
    return jnp.where(colour_mask, update, field_ext[:, 1:-1])


def parity(planes, cells_y, cells_z, first_plane):
    plane_x = first_plane + lax.iota(jnp.int32, planes)
    plane_y = lax.iota(jnp.int32, cells_y)
    plane_z = lax.iota(jnp.int32, cells_z)
    summed = plane_x[:, None, None] + plane_y[None, :, None] + plane_z[None, None, :]
    return summed % 2 == 0


def pad_rows(field_now, width):
    return jnp.pad(field_now, ((0, 0), (width, width), (0, 0), (0, 0)))


def coarsen(array):
    size_x, size_y, size_z = array.shape[-3:]
    leading = array.shape[:-3]
    blocks = array.reshape(leading + (size_x // 2, 2, size_y // 2, 2, size_z // 2, 2))
    return blocks.mean(axis=(-5, -3, -1))


def refine(array):
    return jnp.repeat(jnp.repeat(jnp.repeat(array, 2, axis=-3), 2, axis=-2), 2, axis=-1)


def pairing(forward_ext, adjoint_ext):
    forward_mid = shifted(forward_ext, (0, 0, 0))
    adjoint_mid = shifted(adjoint_ext, (0, 0, 0))
    summed = jnp.zeros(forward_mid.shape, jnp.float32)
    for step in OFFSETS:
        summed = summed + (forward_mid - shifted(forward_ext, step)) * (adjoint_mid - shifted(adjoint_ext, step))
    return -0.5 * jnp.sum(summed, axis=0)


def sweep(field_now, right_side, grid_level, from_zero):
    coupled, diagonal, red_mask = grid_level
    if from_zero:
        field_now = jnp.where(red_mask, right_side / diagonal, 0.0)
    else:
        field_now = relax(pad_rows(field_now, 1), right_side, coupled, diagonal, red_mask)
    return relax(pad_rows(field_now, 1), right_side, coupled, diagonal, jnp.logical_not(red_mask))


def residual_of(field_now, right_side, grid_level):
    coupled, diagonal, red_mask = grid_level
    return right_side - (diagonal * field_now - neighbours(pad_rows(field_now, 1), coupled))


def cycle(levels, level_index, right_side, field_now, from_zero):
    grid_level = levels[level_index]
    if level_index == len(levels) - 1:
        for sweep_index in range(COARSE_SWEEPS):
            field_now = sweep(field_now, right_side, grid_level, sweep_index == 0)
        return field_now
    field_now = sweep(field_now, right_side, grid_level, from_zero)
    coarse_rhs = coarsen(residual_of(field_now, right_side, grid_level))
    correction = cycle(levels, level_index + 1, coarse_rhs, None, True)
    field_now = field_now + refine(correction)
    return sweep(field_now, right_side, grid_level, False)


def reference(conductivity, prior_potential, electrodes, currents, receivers, observed):
    levels = []
    sigma_level = conductivity
    for level_index in range(LEVELS):
        weight = 0.25 ** level_index
        planes, cells_y, cells_z = sigma_level.shape
        coupled = couplings(jnp.pad(sigma_level, ((1, 1), (0, 0), (0, 0))), weight)
        levels.append((coupled, diagonal_of(coupled), parity(planes, cells_y, cells_z, 0)))
        if level_index < LEVELS - 1:
            sigma_level = coarsen(sigma_level)
    source_rows = jnp.arange(NSRC, dtype=jnp.int32)
    source = jnp.zeros((NSRC, NCELLS), jnp.float32)
    source = source.at[source_rows, electrodes[:, 0]].add(currents)
    source = source.at[source_rows, electrodes[:, 1]].add(-currents)
    source = source.reshape(NSRC, NX, NY, NZ)
    potential = cycle(levels, 0, source, prior_potential, False)
    at_receivers = potential.reshape(NSRC, NCELLS)[:, receivers]
    misfit = at_receivers - observed
    adjoint_source = jnp.zeros((NSRC, NCELLS), jnp.float32).at[:, receivers].add(misfit)
    adjoint = cycle(levels, 0, adjoint_source.reshape(NSRC, NX, NY, NZ), None, True)
    padding = ((0, 0), (1, 1), (1, 1), (1, 1))
    gradient = pairing(jnp.pad(potential, padding), jnp.pad(adjoint, padding))
    return potential, misfit, gradient
```

```python
import functools

import jax
import jax.numpy as jnp
from jax import lax
from jax.experimental import pallas as pl
from jax.experimental.pallas import tpu as pltpu
from jax.sharding import PartitionSpec as P

LEVELS = 4
COARSE_SWEEPS = 4
SUB = 8
LANES = 128
ROWS = (4, 2, 1, 1)
Y_STEP = (1, 1, 1, 2)
UNROLL = (4, 4, 8, 8)


class Level:
    def __init__(self, index, planes, field, right, couple_x, couple_y, couple_z, diagonal, inverse, sigma):
        self.index, self.planes = index, planes
        self.rows, self.y_step, self.z_step = ROWS[index], Y_STEP[index], 1 << index
        self.field, self.right = field, right
        self.couple_x, self.couple_y, self.couple_z = couple_x, couple_y, couple_z
        self.diagonal, self.inverse, self.sigma = diagonal, inverse, sigma
        self.unroll = min(UNROLL[index], planes)
        lane = lax.broadcasted_iota(jnp.int32, (SUB, LANES), 1)
        sub = lax.broadcasted_iota(jnp.int32, (SUB, LANES), 0)
        self.lane, self.sub = lane, sub
        parity = (lane >> index) & 1
        if index == 2:
            parity = (parity + sub) & 1
        if index == 3:
            parity = (parity + (sub >> 1)) & 1
        self.even = parity == 0
        self.odd = parity == 1
        self.z_even = ((lane >> index) & 1) == 0
        self.last_z = lane >= LANES - self.z_step
        self.last_y = sub >= SUB - self.y_step
        self.first_z = lane < self.z_step
        self.first_y = sub < self.y_step

    def mask(self, plane, row, colour):
        return self.even if (plane + row + colour) % 2 == 0 else self.odd

    def z_up(self, value):
        return pltpu.roll(value, LANES - self.z_step, 1)

    def z_down(self, value):
        return pltpu.roll(value, self.z_step, 1)

    def y_up(self, value):
        return pltpu.roll(value, SUB - self.y_step, 0)

    def y_down(self, value):
        return pltpu.roll(value, self.y_step, 0)


def blocks(level, body, start=None, stop=None):
    count = level.planes // level.unroll
    if start is None and count == 1:
        body(0)
        return
    first = 0 if start is None else start // level.unroll
    last = count if stop is None else stop // level.unroll

    def step(block, carry):
        body(block * level.unroll)
        return carry

    lax.fori_loop(first, last, step, 0)


def setup(level):
    rows = level.rows

    def body(base):
        sig = [[level.sigma[base + p, j] for j in range(rows)] for p in range(level.unroll + 2)]
        for p in range(level.unroll):
            for j in range(rows):
                mid = sig[p + 1][j]
                above = mid + sig[p + 2][j]
                below = mid + sig[p][j]
                if j + 1 < rows:
                    y_above = sig[p + 1][j + 1]
                else:
                    y_above = jnp.where(level.last_y, 0.0, level.y_up(sig[p + 1][0]))
                if j > 0:
                    y_below = sig[p + 1][j - 1]
                else:
                    y_below = jnp.where(level.first_y, 0.0, level.y_down(sig[p + 1][rows - 1]))
                z_above = jnp.where(level.last_z, 0.0, level.z_up(mid))
                z_below = jnp.where(level.first_z, 0.0, level.z_down(mid))
                diagonal = above + below + (4.0 * mid + ((y_above + y_below) + (z_above + z_below)))
                level.couple_x[base + p + 1, j] = above
                if j + 1 < rows:
                    level.couple_y[base + p, j] = mid + y_above
                else:
                    level.couple_y[base + p, j] = jnp.where(level.last_y, 0.0, mid + y_above)
                level.couple_z[base + p, j] = jnp.where(level.last_z, 0.0, mid + z_above)
                level.diagonal[base + p, j] = diagonal
                level.inverse[base + p, j] = 1.0 / diagonal

    for j in range(rows):
        level.couple_x[0, j] = jnp.zeros((SUB, LANES), jnp.float32)
    blocks(level, body)


def gathered(level, field, base):
    rows = level.rows
    planes = [[field[base + p, j] for j in range(rows)] for p in range(level.unroll + 2)]
    couple_x = [[level.couple_x[base + p, j] for j in range(rows)] for p in range(level.unroll + 1)]
    sums = []
    for p in range(level.unroll):
        mid = planes[p + 1]
        couple_y = [level.couple_y[base + p, j] for j in range(rows)]
        row = []
        for j in range(rows):
            couple_z = level.couple_z[base + p, j]
            total = level.right[base + p, j] + couple_x[p + 1][j] * planes[p + 2][j]
            total = total + couple_x[p][j] * planes[p][j]
            y_above = mid[j + 1] if j + 1 < rows else level.y_up(mid[0])
            total = total + couple_y[j] * y_above
            if j > 0:
                total = total + couple_y[j - 1] * mid[j - 1]
            else:
                total = total + level.y_down(couple_y[rows - 1] * mid[rows - 1])
            total = total + (couple_z * level.z_up(mid[j]) + level.z_down(couple_z * mid[j]))
            row.append(total)
        sums.append(row)
    return sums, planes


def half_sweep(level, field, colour, start=None, stop=None):
    def body(base):
        sums, planes = gathered(level, field, base)
        for p in range(level.unroll):
            for j in range(level.rows):
                update = sums[p][j] * level.inverse[base + p, j]
                field[base + p + 1, j] = jnp.where(level.mask(p, j, colour), update, planes[p + 1][j])

    blocks(level, body, start, stop)


def red_from_zero(level, field):
    def body(base):
        for p in range(level.unroll):
            for j in range(level.rows):
                update = level.right[base + p, j] * level.inverse[base + p, j]
                field[base + p + 1, j] = jnp.where(level.mask(p, j, 0), update, 0.0)

    blocks(level, body)


def summed_pairs(level, low, high):
    both = [a + b for a, b in zip(low, high)]
    if level.rows > 1:
        both = [both[j] + both[j + 1] for j in range(0, level.rows, 2)]
    else:
        both = [v + jnp.where((level.sub & 1) == 0, level.y_up(v), level.y_down(v)) for v in both]
    return [v + jnp.where(level.z_even, level.z_up(v), level.z_down(v)) for v in both]


def restrict_residual(level, field, coarse):
    def body(base):
        sums, planes = gathered(level, field, base)
        left = [
            [sums[p][j] - level.diagonal[base + p, j] * planes[p + 1][j] for j in range(level.rows)]
            for p in range(level.unroll)
        ]
        for p in range(0, level.unroll, 2):
            for j, value in enumerate(summed_pairs(level, left[p], left[p + 1])):
                coarse.right[base // 2 + p // 2, j] = 0.5 * value

    blocks(level, body)


def restrict_sigma(level, coarse):
    def body(base):
        for p in range(0, level.unroll, 2):
            low = [level.sigma[base + p + 1, j] for j in range(level.rows)]
            high = [level.sigma[base + p + 2, j] for j in range(level.rows)]
            for j, value in enumerate(summed_pairs(level, low, high)):
                coarse.sigma[base // 2 + p // 2 + 1, j] = 0.125 * value

    blocks(level, body)


def correct(level, field, coarse, start=None, stop=None):
    def body(base):
        for p in range(level.unroll):
            for j in range(level.rows):
                e = coarse.field[base // 2 + p // 2 + 1, j * coarse.rows // level.rows]
                field[base + p + 1, j] = field[base + p + 1, j] + e

    blocks(level, body, start, stop)


def coarse_solve(levels, index):
    level = levels[index]
    if index == len(levels) - 1:
        red_from_zero(level, level.field)
        half_sweep(level, level.field, 1)
        for _ in range(COARSE_SWEEPS - 1):
            half_sweep(level, level.field, 0)
            half_sweep(level, level.field, 1)
        return
    red_from_zero(level, level.field)
    half_sweep(level, level.field, 1)
    restrict_residual(level, level.field, levels[index + 1])
    coarse_solve(levels, index + 1)
    correct(level, level.field, levels[index + 1])
    half_sweep(level, level.field, 0)
    half_sweep(level, level.field, 1)


def cell_of(flat):
    y = (flat >> 7) & 31
    return flat >> 12, y & 3, y >> 2, flat & 127


def kernel(masks, total, ints, currents, observed, *refs):
    parts = len(masks)
    sigma_parts, prior_parts = refs[:parts], refs[parts : 2 * parts]
    potential_out, misfit_out, keep_out, send_out = refs[2 * parts : 2 * parts + 4]
    scratch = list(refs[2 * parts + 4 :])
    forward = scratch.pop(0)
    local = prior_parts[0].shape[1]
    levels = []
    for index in range(LEVELS):
        arrays = [scratch.pop(0) for _ in range(7)]
        sigma = scratch.pop(0) if index else arrays[0]
        levels.append(Level(index, total >> index, *arrays, sigma))
    fine = levels[0]
    adjoint = fine.field
    position, half = ints[0], ints[1]
    receivers = ints.shape[0] - 4
    zero = jnp.zeros((SUB, LANES), jnp.float32)

    for level in levels:
        for ref in [level.field] + ([level.sigma] if level.index else [forward]):
            for j in range(level.rows):
                ref[0, j] = zero
                ref[level.planes + 1, j] = zero

    for mask, sigma_part, prior_part in zip(masks, sigma_parts, prior_parts):
        base = (position ^ mask) * local

        def place(plane, carry, base=base, sigma_part=sigma_part, prior_part=prior_part):
            for j in range(ROWS[0]):
                adjoint[base + plane + 1, j] = sigma_part[plane, pl.ds(j, SUB, stride=4), :]
                forward[base + plane + 1, j] = prior_part[0, plane, pl.ds(j, SUB, stride=4), :]
                fine.right[base + plane, j] = zero
            return carry

        lax.fori_loop(0, local, place, 0, unroll=2)

    setup(fine)
    for index in range(LEVELS - 1):
        restrict_sigma(levels[index], levels[index + 1])
        setup(levels[index + 1])
    for j in range(ROWS[0]):
        adjoint[0, j] = zero
        adjoint[fine.planes + 1, j] = zero

    lane = lax.broadcasted_iota(jnp.int32, (1, LANES), 1)
    for which, sign in ((0, 2.0), (1, -2.0)):
        x, j, s, z = cell_of(ints[2 + which])
        row = fine.right[x, j, pl.ds(s, 1), :]
        fine.right[x, j, pl.ds(s, 1), :] = row + jnp.where(lane == z, sign * currents[0], 0.0)

    half_sweep(fine, forward, 0)
    half_sweep(fine, forward, 1)
    restrict_residual(fine, forward, levels[1])
    coarse_solve(levels, 1)
    correct(fine, forward, levels[1])
    half_sweep(fine, forward, 0)
    half_sweep(fine, forward, 1)

    for which in range(2):
        x, j, s, z = cell_of(ints[2 + which])
        fine.right[x, j, pl.ds(s, 1), :] = jnp.zeros((1, LANES), jnp.float32)

    def receive(k, carry):
        x, j, s, z = cell_of(ints[4 + k])
        value = jnp.where(lane == z, forward[x + 1, j, pl.ds(s, 1), :] - observed[k], 0.0)
        misfit_out[pl.ds(k, 1), :] = value
        fine.right[x, j, pl.ds(s, 1), :] = fine.right[x, j, pl.ds(s, 1), :] + 2.0 * value
        return carry

    lax.fori_loop(0, receivers, receive, 0, unroll=4)

    first = position * local
    margin = fine.unroll
    low = jnp.maximum(first - margin, 0)
    high = jnp.minimum(first + local + margin, fine.planes)
    red_from_zero(fine, adjoint)
    half_sweep(fine, adjoint, 1)
    restrict_residual(fine, adjoint, levels[1])
    coarse_solve(levels, 1)
    correct(fine, adjoint, levels[1], jnp.maximum(low - margin, 0), jnp.minimum(high + margin, fine.planes))
    half_sweep(fine, adjoint, 0, low, high)
    half_sweep(fine, adjoint, 1, low, high)

    def gradient(base, out, out_base):
        def plane_of(plane, carry):
            at = base + plane + 1
            p = [forward[at, j] for j in range(4)]
            a = [adjoint[at, j] for j in range(4)]
            y_pairs = []
            for j in range(4):
                if j < 3:
                    up_p, up_a = p[j + 1], a[j + 1]
                else:
                    up_p = jnp.where(fine.last_y, 0.0, fine.y_up(p[0]))
                    up_a = jnp.where(fine.last_y, 0.0, fine.y_up(a[0]))
                y_pairs.append((p[j] - up_p) * (a[j] - up_a))
            for j in range(4):
                own = p[j] * a[j]
                value = (p[j] - forward[at - 1, j]) * (a[j] - adjoint[at - 1, j])
                value = value + (p[j] - forward[at + 1, j]) * (a[j] - adjoint[at + 1, j])
                if j > 0:
                    y_below = y_pairs[j - 1]
                else:
                    y_below = jnp.where(fine.first_y, own, fine.y_down(y_pairs[3]))
                value = value + (y_pairs[j] + y_below)
                up_p = jnp.where(fine.last_z, 0.0, fine.z_up(p[j]))
                up_a = jnp.where(fine.last_z, 0.0, fine.z_up(a[j]))
                z_pair = (p[j] - up_p) * (a[j] - up_a)
                z_below = jnp.where(fine.first_z, own, fine.z_down(z_pair))
                value = value + (z_pair + z_below)
                out[out_base + plane, pl.ds(j, SUB, stride=4), :] = -0.5 * value
            return carry

        lax.fori_loop(0, local // 2, plane_of, 0, unroll=2)

    def deliver(plane, carry):
        for j in range(4):
            potential_out[0, plane, pl.ds(j, SUB, stride=4), :] = forward[first + plane + 1, j]
        return carry

    gradient(first + half * (local // 2), keep_out, 0)
    gradient(first + (1 - half) * (local // 2), send_out, 0)
    lax.fori_loop(0, local, deliver, 0, unroll=2)


def solve(sigma_parts, prior_parts, masks, ints, currents, observed):
    local, cells_y, cells_z = sigma_parts[0].shape
    parts = len(masks)
    total = local * parts
    receivers = observed.shape[-1]

    def planes(count, index):
        return pltpu.VMEM((count, ROWS[index], SUB, LANES), jnp.float32)

    scratch = [planes(total + 2, 0)]
    for index in range(LEVELS):
        n = total >> index
        scratch += [planes(n + 2, index), planes(n, index), planes(n + 1, index)]
        scratch += [planes(n, index) for _ in range(4)]
        if index:
            scratch.append(planes(n + 2, index))
    held = 4 * sum(s.shape[0] * s.shape[1] * SUB * LANES for s in scratch)
    held += 4 * cells_y * cells_z * local * (2 * parts + 2) + 4 * LANES * receivers
    half = jax.ShapeDtypeStruct((local // 2, cells_y, cells_z), jnp.float32)
    smem = pl.BlockSpec(memory_space=pltpu.SMEM)
    vmem = pl.BlockSpec(memory_space=pltpu.VMEM)
    return pl.pallas_call(
        functools.partial(kernel, masks, total),
        out_shape=(
            jax.ShapeDtypeStruct((1, local, cells_y, cells_z), jnp.float32),
            jax.ShapeDtypeStruct((receivers, LANES), jnp.float32),
            half,
            half,
        ),
        in_specs=[smem] * 3 + [vmem] * (2 * parts),
        out_specs=[vmem] * 4,
        scratch_shapes=scratch,
        compiler_params=pltpu.CompilerParams(vmem_limit_bytes=min(held + (6 << 20), 63 << 20)),
        name="both_cycles",
    )(ints, currents, observed, *sigma_parts, *prior_parts)


def exchanged(value, axis, mask):
    return lax.ppermute(value, axis, [(i, i ^ mask) for i in range(lax.axis_size(axis))])


def body(conductivity, prior_potential, electrodes, currents, receivers, observed):
    count = lax.axis_size("space")
    position = lax.axis_index("space")
    source = lax.axis_index("src")
    sigma_parts, prior_parts, masks = [conductivity], [prior_potential], [0]
    bit = count // 2
    while bit:
        sigma_parts += [exchanged(part, "space", bit) for part in sigma_parts]
        prior_parts += [exchanged(part, "space", bit) for part in prior_parts]
        masks += [mask ^ bit for mask in masks]
        bit //= 2
    upper = source & 1
    ints = jnp.concatenate([jnp.stack([position, upper]), electrodes[0], receivers])
    potential, picked, keep, send = solve(
        sigma_parts, prior_parts, tuple(masks), ints, currents, observed[0]
    )
    misfit = jnp.sum(picked, axis=1)[None, :]
    summed = keep + exchanged(send, "src", 1)
    bit = 2
    while bit < lax.axis_size("src"):
        summed = summed + exchanged(summed, "src", bit)
        bit *= 2
    other = exchanged(summed, "src", 1)
    gradient = jnp.concatenate(
        [jnp.where(upper == 1, other, summed), jnp.where(upper == 1, summed, other)], 0
    )
    return potential, misfit, gradient


def solution(mesh):
    return jax.shard_map(
        body,
        mesh=mesh,
        in_specs=(
            P(("group", "space"), None, None),
            P(("group", "src"), "space", None, None),
            P(("group", "src"), None),
            P(("group", "src")),
            P("group"),
            P(("group", "src"), None),
        ),
        out_specs=(
            P(("group", "src"), "space", None, None),
            P(("group", "src"), None),
            P(("group", "space"), None, None),
        ),
        check_vma=False,
    )
```

```python
import functools

import jax
import jax.numpy as jnp
from jax import lax
from jax.experimental import pallas as pl
from jax.experimental.pallas import tpu as pltpu
from jax.sharding import PartitionSpec as P

LEVELS = 4
COARSE_SWEEPS = 4
SUB = 8
LANES = 128
ROWS = (4, 2, 1, 1)
Y_STEP = (1, 1, 1, 2)
UNROLL = (32, 32, 16, 8)


class Level:
    def __init__(self, index, planes, field, right, couple_x, couple_y, couple_z, diagonal, inverse, sigma):
        self.index, self.planes = index, planes
        self.rows, self.y_step, self.z_step = ROWS[index], Y_STEP[index], 1 << index
        self.field, self.right = field, right
        self.couple_x, self.couple_y, self.couple_z = couple_x, couple_y, couple_z
        self.diagonal, self.inverse, self.sigma = diagonal, inverse, sigma
        self.unroll = min(UNROLL[index], planes)
        lane = lax.broadcasted_iota(jnp.int32, (SUB, LANES), 1)
        sub = lax.broadcasted_iota(jnp.int32, (SUB, LANES), 0)
        self.lane, self.sub = lane, sub
        parity = (lane >> index) & 1
        if index == 2:
            parity = (parity + sub) & 1
        if index == 3:
            parity = (parity + (sub >> 1)) & 1
        self.even = parity == 0
        self.odd = parity == 1
        self.z_even = ((lane >> index) & 1) == 0
        self.last_z = lane >= LANES - self.z_step
        self.last_y = sub >= SUB - self.y_step
        self.first_z = lane < self.z_step
        self.first_y = sub < self.y_step

    def mask(self, plane, row, colour):
        return self.even if (plane + row + colour) % 2 == 0 else self.odd

    def z_up(self, value):
        return pltpu.roll(value, LANES - self.z_step, 1)

    def z_down(self, value):
        return pltpu.roll(value, self.z_step, 1)

    def y_up(self, value):
        return pltpu.roll(value, SUB - self.y_step, 0)

    def y_down(self, value):
        return pltpu.roll(value, self.y_step, 0)


def blocks(level, body, window=None):
    if window is not None:
        body(*window)
        return
    count = level.planes // level.unroll
    if count == 1:
        body(0, level.unroll)
        return

    def step(block, carry):
        body(block * level.unroll, level.unroll)
        return carry

    lax.fori_loop(0, count, step, 0)


def setup(level):
    rows = level.rows

    def body(base, count):
        sig = [[level.sigma[base + p, j] for j in range(rows)] for p in range(count + 2)]
        for p in range(count):
            for j in range(rows):
                mid = sig[p + 1][j]
                above = mid + sig[p + 2][j]
                below = mid + sig[p][j]
                if j + 1 < rows:
                    y_above = sig[p + 1][j + 1]
                else:
                    y_above = jnp.where(level.last_y, 0.0, level.y_up(sig[p + 1][0]))
                if j > 0:
                    y_below = sig[p + 1][j - 1]
                else:
                    y_below = jnp.where(level.first_y, 0.0, level.y_down(sig[p + 1][rows - 1]))
                z_above = jnp.where(level.last_z, 0.0, level.z_up(mid))
                z_below = jnp.where(level.first_z, 0.0, level.z_down(mid))
                diagonal = above + below + (4.0 * mid + ((y_above + y_below) + (z_above + z_below)))
                level.couple_x[base + p + 1, j] = above
                if j + 1 < rows:
                    level.couple_y[base + p, j] = mid + y_above
                else:
                    level.couple_y[base + p, j] = jnp.where(level.last_y, 0.0, mid + y_above)
                level.couple_z[base + p, j] = jnp.where(level.last_z, 0.0, mid + z_above)
                level.diagonal[base + p, j] = diagonal
                level.inverse[base + p, j] = 1.0 / diagonal

    for j in range(rows):
        level.couple_x[0, j] = jnp.zeros((SUB, LANES), jnp.float32)
    blocks(level, body)


def gathered(level, field, base, count):
    rows = level.rows
    planes = [[field[base + p, j] for j in range(rows)] for p in range(count + 2)]
    couple_x = [[level.couple_x[base + p, j] for j in range(rows)] for p in range(count + 1)]
    sums = []
    for p in range(count):
        mid = planes[p + 1]
        couple_y = [level.couple_y[base + p, j] for j in range(rows)]
        row = []
        for j in range(rows):
            couple_z = level.couple_z[base + p, j]
            total = level.right[base + p, j] + couple_x[p + 1][j] * planes[p + 2][j]
            total = total + couple_x[p][j] * planes[p][j]
            y_above = mid[j + 1] if j + 1 < rows else level.y_up(mid[0])
            total = total + couple_y[j] * y_above
            if j > 0:
                total = total + couple_y[j - 1] * mid[j - 1]
            else:
                total = total + level.y_down(couple_y[rows - 1] * mid[rows - 1])
            total = total + (couple_z * level.z_up(mid[j]) + level.z_down(couple_z * mid[j]))
            row.append(total)
        sums.append(row)
    return sums, planes


def half_sweep(level, field, colour, window=None):
    def body(base, count):
        sums, planes = gathered(level, field, base, count)
        for p in range(count):
            for j in range(level.rows):
                update = sums[p][j] * level.inverse[base + p, j]
                field[base + p + 1, j] = jnp.where(level.mask(p, j, colour), update, planes[p + 1][j])

    blocks(level, body, window)


def red_from_zero(level, field):
    def body(base, count):
        for p in range(count):
            for j in range(level.rows):
                update = level.right[base + p, j] * level.inverse[base + p, j]
                field[base + p + 1, j] = jnp.where(level.mask(p, j, 0), update, 0.0)

    blocks(level, body)


def summed_pairs(level, low, high):
    both = [a + b for a, b in zip(low, high)]
    if level.rows > 1:
        both = [both[j] + both[j + 1] for j in range(0, level.rows, 2)]
    else:
        both = [v + jnp.where((level.sub & 1) == 0, level.y_up(v), level.y_down(v)) for v in both]
    return [v + jnp.where(level.z_even, level.z_up(v), level.z_down(v)) for v in both]


def restrict_residual(level, field, coarse):
    def body(base, count):
        sums, planes = gathered(level, field, base, count)
        left = [
            [sums[p][j] - level.diagonal[base + p, j] * planes[p + 1][j] for j in range(level.rows)]
            for p in range(count)
        ]
        for p in range(0, count, 2):
            for j, value in enumerate(summed_pairs(level, left[p], left[p + 1])):
                coarse.right[base // 2 + p // 2, j] = 0.5 * value

    blocks(level, body)


def restrict_sigma(level, coarse):
    def body(base, count):
        for p in range(0, count, 2):
            low = [level.sigma[base + p + 1, j] for j in range(level.rows)]
            high = [level.sigma[base + p + 2, j] for j in range(level.rows)]
            for j, value in enumerate(summed_pairs(level, low, high)):
                coarse.sigma[base // 2 + p // 2 + 1, j] = 0.125 * value

    blocks(level, body)


def correct(level, field, coarse, window=None):
    def body(base, count):
        for p in range(count):
            for j in range(level.rows):
                e = coarse.field[base // 2 + p // 2 + 1, j * coarse.rows // level.rows]
                field[base + p + 1, j] = field[base + p + 1, j] + e

    blocks(level, body, window)


def coarse_solve(levels, index):
    level = levels[index]
    if index == len(levels) - 1:
        red_from_zero(level, level.field)
        half_sweep(level, level.field, 1)
        for _ in range(COARSE_SWEEPS - 1):
            half_sweep(level, level.field, 0)
            half_sweep(level, level.field, 1)
        return
    red_from_zero(level, level.field)
    half_sweep(level, level.field, 1)
    restrict_residual(level, level.field, levels[index + 1])
    coarse_solve(levels, index + 1)
    correct(level, level.field, levels[index + 1])
    half_sweep(level, level.field, 0)
    half_sweep(level, level.field, 1)


def cell_of(flat):
    y = (flat >> 7) & 31
    return flat >> 12, y & 3, y >> 2, flat & 127


def kernel(masks, total, ints, currents, observed, *refs):
    parts = len(masks)
    sigma_parts, prior_parts = refs[:parts], refs[parts : 2 * parts]
    potential_out, misfit_out, keep_out, send_out = refs[2 * parts : 2 * parts + 4]
    scratch = list(refs[2 * parts + 4 :])
    forward = scratch.pop(0)
    local = prior_parts[0].shape[1]
    levels = []
    for index in range(LEVELS):
        arrays = [scratch.pop(0) for _ in range(7)]
        sigma = scratch.pop(0) if index else arrays[0]
        levels.append(Level(index, total >> index, *arrays, sigma))
    fine = levels[0]
    adjoint = fine.field
    position, half = ints[0], ints[1]
    receivers = ints.shape[0] - 4
    zero = jnp.zeros((SUB, LANES), jnp.float32)

    for level in levels:
        for ref in [level.field] + ([level.sigma] if level.index else [forward]):
            for j in range(level.rows):
                ref[0, j] = zero
                ref[level.planes + 1, j] = zero

    for mask, sigma_part, prior_part in zip(masks, sigma_parts, prior_parts):
        base = (position ^ mask) * local

        def place(plane, carry, base=base, sigma_part=sigma_part, prior_part=prior_part):
            for j in range(ROWS[0]):
                adjoint[base + plane + 1, j] = sigma_part[plane, pl.ds(j, SUB, stride=4), :]
                forward[base + plane + 1, j] = prior_part[0, plane, pl.ds(j, SUB, stride=4), :]
                fine.right[base + plane, j] = zero
            return carry

        lax.fori_loop(0, local, place, 0, unroll=16)

    setup(fine)
    for index in range(LEVELS - 1):
        restrict_sigma(levels[index], levels[index + 1])
        setup(levels[index + 1])
    for j in range(ROWS[0]):
        adjoint[0, j] = zero
        adjoint[fine.planes + 1, j] = zero

    lane = lax.broadcasted_iota(jnp.int32, (1, LANES), 1)
    for which, sign in ((0, 2.0), (1, -2.0)):
        x, j, s, z = cell_of(ints[2 + which])
        row = fine.right[x, j, pl.ds(s, 1), :]
        fine.right[x, j, pl.ds(s, 1), :] = row + jnp.where(lane == z, sign * currents[0], 0.0)

    half_sweep(fine, forward, 0)
    half_sweep(fine, forward, 1)
    restrict_residual(fine, forward, levels[1])
    coarse_solve(levels, 1)
    correct(fine, forward, levels[1])
    half_sweep(fine, forward, 0)
    half_sweep(fine, forward, 1)

    for which in range(2):
        x, j, s, z = cell_of(ints[2 + which])
        fine.right[x, j, pl.ds(s, 1), :] = jnp.zeros((1, LANES), jnp.float32)

    def receive(k, carry):
        x, j, s, z = cell_of(ints[4 + k])
        value = jnp.where(lane == z, forward[x + 1, j, pl.ds(s, 1), :] - observed[k], 0.0)
        misfit_out[pl.ds(k, 1), :] = value
        fine.right[x, j, pl.ds(s, 1), :] = fine.right[x, j, pl.ds(s, 1), :] + 2.0 * value
        return carry

    lax.fori_loop(0, receivers, receive, 0, unroll=32)

    first = position * local

    def window(margin):
        count = min(local + 2 * margin, fine.planes)
        return jnp.clip(first - margin, 0, fine.planes - count), count

    red_from_zero(fine, adjoint)
    half_sweep(fine, adjoint, 1)
    restrict_residual(fine, adjoint, levels[1])
    coarse_solve(levels, 1)
    correct(fine, adjoint, levels[1], window(4))
    half_sweep(fine, adjoint, 0, window(2))
    half_sweep(fine, adjoint, 1, window(2))

    def gradient(base, out, out_base):
        def plane_of(plane, carry):
            at = base + plane + 1
            p = [forward[at, j] for j in range(4)]
            a = [adjoint[at, j] for j in range(4)]
            y_pairs = []
            for j in range(4):
                if j < 3:
                    up_p, up_a = p[j + 1], a[j + 1]
                else:
                    up_p = jnp.where(fine.last_y, 0.0, fine.y_up(p[0]))
                    up_a = jnp.where(fine.last_y, 0.0, fine.y_up(a[0]))
                y_pairs.append((p[j] - up_p) * (a[j] - up_a))
            for j in range(4):
                own = p[j] * a[j]
                value = (p[j] - forward[at - 1, j]) * (a[j] - adjoint[at - 1, j])
                value = value + (p[j] - forward[at + 1, j]) * (a[j] - adjoint[at + 1, j])
                if j > 0:
                    y_below = y_pairs[j - 1]
                else:
                    y_below = jnp.where(fine.first_y, own, fine.y_down(y_pairs[3]))
                value = value + (y_pairs[j] + y_below)
                up_p = jnp.where(fine.last_z, 0.0, fine.z_up(p[j]))
                up_a = jnp.where(fine.last_z, 0.0, fine.z_up(a[j]))
                z_pair = (p[j] - up_p) * (a[j] - up_a)
                z_below = jnp.where(fine.first_z, own, fine.z_down(z_pair))
                value = value + (z_pair + z_below)
                out[out_base + plane, pl.ds(j, SUB, stride=4), :] = -0.5 * value
            return carry

        lax.fori_loop(0, local // 2, plane_of, 0, unroll=8)

    def deliver(plane, carry):
        for j in range(4):
            potential_out[0, plane, pl.ds(j, SUB, stride=4), :] = forward[first + plane + 1, j]
        return carry

    gradient(first + half * (local // 2), keep_out, 0)
    gradient(first + (1 - half) * (local // 2), send_out, 0)
    lax.fori_loop(0, local, deliver, 0, unroll=16)


def solve(sigma_parts, prior_parts, masks, ints, currents, observed):
    local, cells_y, cells_z = sigma_parts[0].shape
    parts = len(masks)
    total = local * parts
    receivers = observed.shape[-1]

    def planes(count, index):
        return pltpu.VMEM((count, ROWS[index], SUB, LANES), jnp.float32)

    scratch = [planes(total + 2, 0)]
    for index in range(LEVELS):
        n = total >> index
        scratch += [planes(n + 2, index), planes(n, index), planes(n + 1, index)]
        scratch += [planes(n, index) for _ in range(4)]
        if index:
            scratch.append(planes(n + 2, index))
    held = 4 * sum(s.shape[0] * s.shape[1] * SUB * LANES for s in scratch)
    held += 4 * cells_y * cells_z * local * (2 * parts + 2) + 4 * LANES * receivers
    half = jax.ShapeDtypeStruct((local // 2, cells_y, cells_z), jnp.float32)
    smem = pl.BlockSpec(memory_space=pltpu.SMEM)
    vmem = pl.BlockSpec(memory_space=pltpu.VMEM)
    return pl.pallas_call(
        functools.partial(kernel, masks, total),
        out_shape=(
            jax.ShapeDtypeStruct((1, local, cells_y, cells_z), jnp.float32),
            jax.ShapeDtypeStruct((receivers, LANES), jnp.float32),
            half,
            half,
        ),
        in_specs=[smem] * 3 + [vmem] * (2 * parts),
        out_specs=[vmem] * 4,
        scratch_shapes=scratch,
        compiler_params=pltpu.CompilerParams(vmem_limit_bytes=min(held + (6 << 20), 63 << 20)),
        name="both_cycles",
    )(ints, currents, observed, *sigma_parts, *prior_parts)


def exchanged(value, axis, mask):
    return lax.ppermute(value, axis, [(i, i ^ mask) for i in range(lax.axis_size(axis))])


def body(conductivity, prior_potential, electrodes, currents, receivers, observed):
    count = lax.axis_size("space")
    position = lax.axis_index("space")
    source = lax.axis_index("src")
    sigma_parts, prior_parts, masks = [conductivity], [prior_potential], [0]
    bit = count // 2
    while bit:
        sigma_parts += [exchanged(part, "space", bit) for part in sigma_parts]
        prior_parts += [exchanged(part, "space", bit) for part in prior_parts]
        masks += [mask ^ bit for mask in masks]
        bit //= 2
    upper = source & 1
    ints = jnp.concatenate([jnp.stack([position, upper]), electrodes[0], receivers])
    potential, picked, keep, send = solve(
        sigma_parts, prior_parts, tuple(masks), ints, currents, observed[0]
    )
    misfit = jnp.sum(picked, axis=1)[None, :]
    summed = keep + exchanged(send, "src", 1)
    bit = 2
    while bit < lax.axis_size("src"):
        summed = summed + exchanged(summed, "src", bit)
        bit *= 2
    other = exchanged(summed, "src", 1)
    gradient = jnp.concatenate(
        [jnp.where(upper == 1, other, summed), jnp.where(upper == 1, summed, other)], 0
    )
    return potential, misfit, gradient


def solution(mesh):
    return jax.shard_map(
        body,
        mesh=mesh,
        in_specs=(
            P(("group", "space"), None, None),
            P(("group", "src"), "space", None, None),
            P(("group", "src"), None),
            P(("group", "src")),
            P("group"),
            P(("group", "src"), None),
        ),
        out_specs=(
            P(("group", "src"), "space", None, None),
            P(("group", "src"), None),
            P(("group", "space"), None, None),
        ),
        check_vma=False,
    )
```

```python
import functools

import jax
import jax.numpy as jnp
from jax import lax
from jax.experimental import pallas as pl
from jax.experimental.pallas import tpu as pltpu
from jax.sharding import PartitionSpec as P

LEVELS = 4
COARSE_SWEEPS = 4
SUB = 8
LANES = 128
ROWS = (4, 2, 1, 1)
Y_STEP = (1, 1, 1, 2)
UNROLL = (32, 32, 16, 8)


class Level:
    def __init__(self, index, planes, field, right, couple_x, couple_y, couple_z, diagonal, inverse, sigma):
        self.index, self.planes = index, planes
        self.rows, self.y_step, self.z_step = ROWS[index], Y_STEP[index], 1 << index
        self.field, self.right = field, right
        self.couple_x, self.couple_y, self.couple_z = couple_x, couple_y, couple_z
        self.diagonal, self.inverse, self.sigma = diagonal, inverse, sigma
        self.unroll = min(UNROLL[index], planes)
        lane = lax.broadcasted_iota(jnp.int32, (SUB, LANES), 1)
        sub = lax.broadcasted_iota(jnp.int32, (SUB, LANES), 0)
        self.lane, self.sub = lane, sub
        parity = (lane >> index) & 1
        if index == 2:
            parity = (parity + sub) & 1
        if index == 3:
            parity = (parity + (sub >> 1)) & 1
        self.even = parity == 0
        self.odd = parity == 1
        self.z_even = ((lane >> index) & 1) == 0
        self.last_z = lane >= LANES - self.z_step
        self.last_y = sub >= SUB - self.y_step
        self.first_z = lane < self.z_step
        self.first_y = sub < self.y_step

    def mask(self, plane, row, colour):
        return self.even if (plane + row + colour) % 2 == 0 else self.odd

    def z_up(self, value):
        return pltpu.roll(value, LANES - self.z_step, 1)

    def z_down(self, value):
        return pltpu.roll(value, self.z_step, 1)

    def y_up(self, value):
        return pltpu.roll(value, SUB - self.y_step, 0)

    def y_down(self, value):
        return pltpu.roll(value, self.y_step, 0)


def blocks(level, body, window=None):
    if window is not None:
        body(*window)
        return
    count = level.planes // level.unroll
    if count == 1:
        body(0, level.unroll)
        return

    def step(block, carry):
        body(block * level.unroll, level.unroll)
        return carry

    lax.fori_loop(0, count, step, 0)


def setup(level):
    rows = level.rows

    def body(base, count):
        sig = [[level.sigma[base + p, j] for j in range(rows)] for p in range(count + 2)]
        for p in range(count):
            for j in range(rows):
                mid = sig[p + 1][j]
                above = mid + sig[p + 2][j]
                below = mid + sig[p][j]
                if j + 1 < rows:
                    y_above = sig[p + 1][j + 1]
                else:
                    y_above = jnp.where(level.last_y, 0.0, level.y_up(sig[p + 1][0]))
                if j > 0:
                    y_below = sig[p + 1][j - 1]
                else:
                    y_below = jnp.where(level.first_y, 0.0, level.y_down(sig[p + 1][rows - 1]))
                z_above = jnp.where(level.last_z, 0.0, level.z_up(mid))
                z_below = jnp.where(level.first_z, 0.0, level.z_down(mid))
                diagonal = above + below + (4.0 * mid + ((y_above + y_below) + (z_above + z_below)))
                level.couple_x[base + p + 1, j] = above
                if j + 1 < rows:
                    level.couple_y[base + p, j] = mid + y_above
                else:
                    level.couple_y[base + p, j] = jnp.where(level.last_y, 0.0, mid + y_above)
                level.couple_z[base + p, j] = jnp.where(level.last_z, 0.0, mid + z_above)
                level.diagonal[base + p, j] = diagonal
                level.inverse[base + p, j] = 1.0 / diagonal

    for j in range(rows):
        level.couple_x[0, j] = jnp.zeros((SUB, LANES), jnp.float32)
    blocks(level, body)


def gathered(level, field, base, count):
    rows = level.rows
    planes = [[field[base + p, j] for j in range(rows)] for p in range(count + 2)]
    couple_x = [[level.couple_x[base + p, j] for j in range(rows)] for p in range(count + 1)]
    sums = []
    for p in range(count):
        mid = planes[p + 1]
        couple_y = [level.couple_y[base + p, j] for j in range(rows)]
        row = []
        for j in range(rows):
            couple_z = level.couple_z[base + p, j]
            total = level.right[base + p, j] + couple_x[p + 1][j] * planes[p + 2][j]
            total = total + couple_x[p][j] * planes[p][j]
            y_above = mid[j + 1] if j + 1 < rows else level.y_up(mid[0])
            total = total + couple_y[j] * y_above
            if j > 0:
                total = total + couple_y[j - 1] * mid[j - 1]
            else:
                total = total + level.y_down(couple_y[rows - 1] * mid[rows - 1])
            total = total + (couple_z * level.z_up(mid[j]) + level.z_down(couple_z * mid[j]))
            row.append(total)
        sums.append(row)
    return sums, planes


def half_sweep(level, field, colour, window=None):
    def body(base, count):
        sums, planes = gathered(level, field, base, count)
        for p in range(count):
            for j in range(level.rows):
                update = sums[p][j] * level.inverse[base + p, j]
                field[base + p + 1, j] = jnp.where(level.mask(p, j, colour), update, planes[p + 1][j])

    blocks(level, body, window)


def red_from_zero(level, field):
    def body(base, count):
        for p in range(count):
            for j in range(level.rows):
                update = level.right[base + p, j] * level.inverse[base + p, j]
                field[base + p + 1, j] = jnp.where(level.mask(p, j, 0), update, 0.0)

    blocks(level, body)


def summed_pairs(level, low, high):
    both = [a + b for a, b in zip(low, high)]
    if level.rows > 1:
        both = [both[j] + both[j + 1] for j in range(0, level.rows, 2)]
    else:
        both = [v + jnp.where((level.sub & 1) == 0, level.y_up(v), level.y_down(v)) for v in both]
    return [v + jnp.where(level.z_even, level.z_up(v), level.z_down(v)) for v in both]


def restrict_residual(level, field, coarse):
    def body(base, count):
        sums, planes = gathered(level, field, base, count)
        left = [
            [sums[p][j] - level.diagonal[base + p, j] * planes[p + 1][j] for j in range(level.rows)]
            for p in range(count)
        ]
        for p in range(0, count, 2):
            for j, value in enumerate(summed_pairs(level, left[p], left[p + 1])):
                coarse.right[base // 2 + p // 2, j] = 0.5 * value

    blocks(level, body)


def restrict_sigma(level, coarse):
    def body(base, count):
        for p in range(0, count, 2):
            low = [level.sigma[base + p + 1, j] for j in range(level.rows)]
            high = [level.sigma[base + p + 2, j] for j in range(level.rows)]
            for j, value in enumerate(summed_pairs(level, low, high)):
                coarse.sigma[base // 2 + p // 2 + 1, j] = 0.125 * value

    blocks(level, body)


def correct(level, field, coarse, window=None):
    def body(base, count):
        for p in range(count):
            for j in range(level.rows):
                e = coarse.field[base // 2 + p // 2 + 1, j * coarse.rows // level.rows]
                field[base + p + 1, j] = field[base + p + 1, j] + e

    blocks(level, body, window)


def coarse_solve(levels, index):
    level = levels[index]
    if index == len(levels) - 1:
        red_from_zero(level, level.field)
        half_sweep(level, level.field, 1)
        for _ in range(COARSE_SWEEPS - 1):
            half_sweep(level, level.field, 0)
            half_sweep(level, level.field, 1)
        return
    red_from_zero(level, level.field)
    half_sweep(level, level.field, 1)
    restrict_residual(level, level.field, levels[index + 1])
    coarse_solve(levels, index + 1)
    correct(level, level.field, levels[index + 1])
    half_sweep(level, level.field, 0)
    half_sweep(level, level.field, 1)


def cell_of(flat):
    y = (flat >> 7) & 31
    return flat >> 12, y & 3, y >> 2, flat & 127


def kernel(masks, total, ints, currents, observed, *refs):
    parts = len(masks)
    sigma_parts, prior_parts = refs[:parts], refs[parts : 2 * parts]
    potential_out, misfit_out, low_out, high_out = refs[2 * parts : 2 * parts + 4]
    scratch = list(refs[2 * parts + 4 :])
    sigma_own, prior_own, staged, arrived, left = [scratch.pop(0) for _ in range(5)]
    sigma_copy = pltpu.make_async_copy(sigma_parts[0], sigma_own, arrived.at[0])
    prior_copy = pltpu.make_async_copy(prior_parts[0], prior_own, arrived.at[1])
    sigma_copy.start()
    prior_copy.start()
    forward = scratch.pop(0)
    local = prior_parts[0].shape[1]
    levels = []
    for index in range(LEVELS):
        arrays = [scratch.pop(0) for _ in range(7)]
        sigma = scratch.pop(0) if index else arrays[0]
        levels.append(Level(index, total >> index, *arrays, sigma))
    fine = levels[0]
    adjoint = fine.field
    position = ints[0]
    receivers = ints.shape[0] - 3
    zero = jnp.zeros((SUB, LANES), jnp.float32)

    for level in levels:
        for ref in [level.field] + ([level.sigma] if level.index else [forward]):
            for j in range(level.rows):
                ref[0, j] = zero
                ref[level.planes + 1, j] = zero

    for mask, sigma_part, prior_part in reversed(list(zip(masks, sigma_parts, prior_parts))):
        if mask == 0:
            sigma_copy.wait()
            prior_copy.wait()
            sigma_part, prior_part = sigma_own, prior_own
        base = (position ^ mask) * local

        def place(plane, carry, base=base, sigma_part=sigma_part, prior_part=prior_part):
            for j in range(ROWS[0]):
                adjoint[base + plane + 1, j] = sigma_part[plane, pl.ds(j, SUB, stride=4), :]
                forward[base + plane + 1, j] = prior_part[0, plane, pl.ds(j, SUB, stride=4), :]
                fine.right[base + plane, j] = zero
            return carry

        lax.fori_loop(0, local, place, 0, unroll=16)

    setup(fine)
    for index in range(LEVELS - 1):
        restrict_sigma(levels[index], levels[index + 1])
        setup(levels[index + 1])
    for j in range(ROWS[0]):
        adjoint[0, j] = zero
        adjoint[fine.planes + 1, j] = zero

    lane = lax.broadcasted_iota(jnp.int32, (1, LANES), 1)
    for which, sign in ((0, 2.0), (1, -2.0)):
        x, j, s, z = cell_of(ints[1 + which])
        row = fine.right[x, j, pl.ds(s, 1), :]
        fine.right[x, j, pl.ds(s, 1), :] = row + jnp.where(lane == z, sign * currents[0], 0.0)

    half_sweep(fine, forward, 0)
    half_sweep(fine, forward, 1)
    restrict_residual(fine, forward, levels[1])
    coarse_solve(levels, 1)
    correct(fine, forward, levels[1])
    half_sweep(fine, forward, 0)
    half_sweep(fine, forward, 1)

    first = position * local

    def deliver(plane, carry):
        for j in range(4):
            staged[0, plane, pl.ds(j, SUB, stride=4), :] = forward[first + plane + 1, j]
        return carry

    lax.fori_loop(0, local, deliver, 0, unroll=16)
    potential_copy = pltpu.make_async_copy(staged, potential_out, left)
    potential_copy.start()

    for which in range(2):
        x, j, s, z = cell_of(ints[1 + which])
        fine.right[x, j, pl.ds(s, 1), :] = jnp.zeros((1, LANES), jnp.float32)

    def receive(k, carry):
        x, j, s, z = cell_of(ints[3 + k])
        value = jnp.where(lane == z, forward[x + 1, j, pl.ds(s, 1), :] - observed[0, k], 0.0)
        misfit_out[pl.ds(k, 1), :] = value
        fine.right[x, j, pl.ds(s, 1), :] = fine.right[x, j, pl.ds(s, 1), :] + 2.0 * value
        return carry

    lax.fori_loop(0, receivers, receive, 0, unroll=32)

    def window(margin):
        count = min(local + 2 * margin, fine.planes)
        return jnp.clip(first - margin, 0, fine.planes - count), count

    red_from_zero(fine, adjoint)
    half_sweep(fine, adjoint, 1)
    restrict_residual(fine, adjoint, levels[1])
    coarse_solve(levels, 1)
    correct(fine, adjoint, levels[1], window(4))
    half_sweep(fine, adjoint, 0, window(2))
    half_sweep(fine, adjoint, 1, window(2))

    def gradient(base, out, out_base):
        def plane_of(plane, carry):
            at = base + plane + 1
            p = [forward[at, j] for j in range(4)]
            a = [adjoint[at, j] for j in range(4)]
            y_pairs = []
            for j in range(4):
                if j < 3:
                    up_p, up_a = p[j + 1], a[j + 1]
                else:
                    up_p = jnp.where(fine.last_y, 0.0, fine.y_up(p[0]))
                    up_a = jnp.where(fine.last_y, 0.0, fine.y_up(a[0]))
                y_pairs.append((p[j] - up_p) * (a[j] - up_a))
            for j in range(4):
                own = p[j] * a[j]
                value = (p[j] - forward[at - 1, j]) * (a[j] - adjoint[at - 1, j])
                value = value + (p[j] - forward[at + 1, j]) * (a[j] - adjoint[at + 1, j])
                if j > 0:
                    y_below = y_pairs[j - 1]
                else:
                    y_below = jnp.where(fine.first_y, own, fine.y_down(y_pairs[3]))
                value = value + (y_pairs[j] + y_below)
                up_p = jnp.where(fine.last_z, 0.0, fine.z_up(p[j]))
                up_a = jnp.where(fine.last_z, 0.0, fine.z_up(a[j]))
                z_pair = (p[j] - up_p) * (a[j] - up_a)
                z_below = jnp.where(fine.first_z, own, fine.z_down(z_pair))
                value = value + (z_pair + z_below)
                out[out_base + plane, pl.ds(j, SUB, stride=4), :] = -0.5 * value
            return carry

        lax.fori_loop(0, local // 2, plane_of, 0, unroll=8)

    gradient(first, low_out, 0)
    gradient(first + local // 2, high_out, 0)
    potential_copy.wait()


def solve(sigma_parts, prior_parts, masks, ints, currents, observed):
    local, cells_y, cells_z = sigma_parts[0].shape
    parts = len(masks)
    total = local * parts
    receivers = observed.shape[-1]

    def planes(count, index):
        return pltpu.VMEM((count, ROWS[index], SUB, LANES), jnp.float32)

    slab = (local, cells_y, cells_z)
    scratch = [pltpu.VMEM(slab, jnp.float32), pltpu.VMEM((1, *slab), jnp.float32), pltpu.VMEM((1, *slab), jnp.float32)]
    scratch += [pltpu.SemaphoreType.DMA((2,)), pltpu.SemaphoreType.DMA, planes(total + 2, 0)]
    for index in range(LEVELS):
        n = total >> index
        scratch += [planes(n + 2, index), planes(n, index), planes(n + 1, index)]
        scratch += [planes(n, index) for _ in range(4)]
        if index:
            scratch.append(planes(n + 2, index))
    held = 4 * sum(s.shape[0] * s.shape[1] * SUB * LANES for s in scratch[5:])
    held += 4 * cells_y * cells_z * local * (2 * parts + 3) + 4 * LANES * receivers
    half = jax.ShapeDtypeStruct((local // 2, cells_y, cells_z), jnp.float32)
    smem = pl.BlockSpec(memory_space=pltpu.SMEM)
    vmem = pl.BlockSpec(memory_space=pltpu.VMEM)
    anywhere = pl.BlockSpec(memory_space=pl.ANY)
    return pl.pallas_call(
        functools.partial(kernel, masks, total),
        out_shape=(
            jax.ShapeDtypeStruct((1, local, cells_y, cells_z), jnp.float32),
            jax.ShapeDtypeStruct((receivers, LANES), jnp.float32),
            half,
            half,
        ),
        in_specs=[smem] * 3 + ([anywhere] + [vmem] * (parts - 1)) * 2,
        out_specs=[anywhere] + [vmem] * 3,
        scratch_shapes=scratch,
        compiler_params=pltpu.CompilerParams(vmem_limit_bytes=min(held + (6 << 20), 63 << 20)),
        name="both_cycles",
    )(ints, currents, observed, *sigma_parts, *prior_parts)


def exchanged(value, axis, mask):
    return lax.ppermute(value, axis, [(i, i ^ mask) for i in range(lax.axis_size(axis))])


def body(conductivity, prior_potential, electrodes, currents, receivers, observed):
    count = lax.axis_size("space")
    position = lax.axis_index("space")
    sigma_parts, prior_parts, masks = [conductivity], [prior_potential], [0]
    bit = count // 2
    while bit:
        sigma_parts += [exchanged(part, "space", bit) for part in sigma_parts]
        prior_parts += [exchanged(part, "space", bit) for part in prior_parts]
        masks += [mask ^ bit for mask in masks]
        bit //= 2
    ints = jnp.concatenate([position[None], electrodes[0], receivers])
    potential, picked, low, high = solve(
        sigma_parts, prior_parts, tuple(masks), ints, currents, observed
    )
    misfit = jnp.sum(picked, axis=1)[None, :]
    orders = [[1], [1]]
    while orders[0][-1] < lax.axis_size("src") - 1:
        step = 2 * orders[0][-1] + 1
        orders = [orders[0] + [step], orders[1][:-1] + [step, orders[1][-1]]]
    for step_low, step_high in zip(*orders):
        from_low = exchanged(low, "src", step_low)
        from_high = exchanged(high, "src", step_high)
        low, high = low + from_low, high + from_high
    return potential, misfit, jnp.concatenate([low, high], 0)


def solution(mesh):
    return jax.shard_map(
        body,
        mesh=mesh,
        in_specs=(
            P(("group", "space"), None, None),
            P(("group", "src"), "space", None, None),
            P(("group", "src"), None),
            P(("group", "src")),
            P("group"),
            P(("group", "src"), None),
        ),
        out_specs=(
            P(("group", "src"), "space", None, None),
            P(("group", "src"), None),
            P(("group", "space"), None, None),
        ),
        check_vma=False,
    )
```

```python
import functools
import math

import jax
import jax.numpy as jnp
from jax import lax
from jax.experimental import pallas as pl
from jax.experimental.pallas import tpu as pltpu
from jax.sharding import PartitionSpec as P

LEVELS = 4
COARSE_SWEEPS = 4
SUB = 8
LANES = 128
ROWS = (4, 2, 1, 1)
Y_STEP = (1, 1, 1, 2)
UNROLL = (32, 32, 16, 8)


class Level:
    def __init__(self, index, planes, field, right, couple_x, couple_y, couple_z, diagonal, inverse, sigma):
        self.index, self.planes = index, planes
        self.rows, self.y_step, self.z_step = ROWS[index], Y_STEP[index], 1 << index
        self.field, self.right = field, right
        self.couple_x, self.couple_y, self.couple_z = couple_x, couple_y, couple_z
        self.diagonal, self.inverse, self.sigma = diagonal, inverse, sigma
        self.unroll = min(UNROLL[index], planes)
        lane = lax.broadcasted_iota(jnp.int32, (SUB, LANES), 1)
        sub = lax.broadcasted_iota(jnp.int32, (SUB, LANES), 0)
        self.lane, self.sub = lane, sub
        parity = (lane >> index) & 1
        if index == 2:
            parity = (parity + sub) & 1
        if index == 3:
            parity = (parity + (sub >> 1)) & 1
        self.even = parity == 0
        self.odd = parity == 1
        self.z_even = ((lane >> index) & 1) == 0
        self.last_z = lane >= LANES - self.z_step
        self.last_y = sub >= SUB - self.y_step
        self.first_z = lane < self.z_step
        self.first_y = sub < self.y_step

    def mask(self, plane, row, colour):
        return self.even if (plane + row + colour) % 2 == 0 else self.odd

    def z_up(self, value):
        return pltpu.roll(value, LANES - self.z_step, 1)

    def z_down(self, value):
        return pltpu.roll(value, self.z_step, 1)

    def y_up(self, value):
        return pltpu.roll(value, SUB - self.y_step, 0)

    def y_down(self, value):
        return pltpu.roll(value, self.y_step, 0)


def blocks(level, body, window=None):
    if window is not None:
        body(*window)
        return
    count = level.planes // level.unroll
    if count == 1:
        body(0, level.unroll)
        return

    def step(block, carry):
        body(block * level.unroll, level.unroll)
        return carry

    lax.fori_loop(0, count, step, 0)


def setup(level):
    rows = level.rows

    def body(base, count):
        sig = [[level.sigma[base + p, j] for j in range(rows)] for p in range(count + 2)]
        for p in range(count):
            for j in range(rows):
                mid = sig[p + 1][j]
                above = mid + sig[p + 2][j]
                below = mid + sig[p][j]
                if j + 1 < rows:
                    y_above = sig[p + 1][j + 1]
                else:
                    y_above = jnp.where(level.last_y, 0.0, level.y_up(sig[p + 1][0]))
                if j > 0:
                    y_below = sig[p + 1][j - 1]
                else:
                    y_below = jnp.where(level.first_y, 0.0, level.y_down(sig[p + 1][rows - 1]))
                z_above = jnp.where(level.last_z, 0.0, level.z_up(mid))
                z_below = jnp.where(level.first_z, 0.0, level.z_down(mid))
                diagonal = above + below + (4.0 * mid + ((y_above + y_below) + (z_above + z_below)))
                level.couple_x[base + p + 1, j] = above
                if j + 1 < rows:
                    level.couple_y[base + p, j] = mid + y_above
                else:
                    level.couple_y[base + p, j] = jnp.where(level.last_y, 0.0, mid + y_above)
                level.couple_z[base + p, j] = jnp.where(level.last_z, 0.0, mid + z_above)
                level.diagonal[base + p, j] = diagonal
                level.inverse[base + p, j] = 1.0 / diagonal

    for j in range(rows):
        level.couple_x[0, j] = jnp.zeros((SUB, LANES), jnp.float32)
    blocks(level, body)


def gathered(level, field, base, count):
    rows = level.rows
    planes = [[field[base + p, j] for j in range(rows)] for p in range(count + 2)]
    couple_x = [[level.couple_x[base + p, j] for j in range(rows)] for p in range(count + 1)]
    sums = []
    for p in range(count):
        mid = planes[p + 1]
        couple_y = [level.couple_y[base + p, j] for j in range(rows)]
        row = []
        for j in range(rows):
            couple_z = level.couple_z[base + p, j]
            total = level.right[base + p, j] + couple_x[p + 1][j] * planes[p + 2][j]
            total = total + couple_x[p][j] * planes[p][j]
            y_above = mid[j + 1] if j + 1 < rows else level.y_up(mid[0])
            total = total + couple_y[j] * y_above
            if j > 0:
                total = total + couple_y[j - 1] * mid[j - 1]
            else:
                total = total + level.y_down(couple_y[rows - 1] * mid[rows - 1])
            total = total + (couple_z * level.z_up(mid[j]) + level.z_down(couple_z * mid[j]))
            row.append(total)
        sums.append(row)
    return sums, planes


def half_sweep(level, field, colour, window=None):
    def body(base, count):
        sums, planes = gathered(level, field, base, count)
        for p in range(count):
            for j in range(level.rows):
                update = sums[p][j] * level.inverse[base + p, j]
                field[base + p + 1, j] = jnp.where(level.mask(p, j, colour), update, planes[p + 1][j])

    blocks(level, body, window)


def red_from_zero(level, field):
    def body(base, count):
        for p in range(count):
            for j in range(level.rows):
                update = level.right[base + p, j] * level.inverse[base + p, j]
                field[base + p + 1, j] = jnp.where(level.mask(p, j, 0), update, 0.0)

    blocks(level, body)


def summed_pairs(level, low, high):
    both = [a + b for a, b in zip(low, high)]
    if level.rows > 1:
        both = [both[j] + both[j + 1] for j in range(0, level.rows, 2)]
    else:
        both = [v + jnp.where((level.sub & 1) == 0, level.y_up(v), level.y_down(v)) for v in both]
    return [v + jnp.where(level.z_even, level.z_up(v), level.z_down(v)) for v in both]


def restrict_residual(level, field, coarse):
    def body(base, count):
        sums, planes = gathered(level, field, base, count)
        left = [
            [sums[p][j] - level.diagonal[base + p, j] * planes[p + 1][j] for j in range(level.rows)]
            for p in range(count)
        ]
        for p in range(0, count, 2):
            for j, value in enumerate(summed_pairs(level, left[p], left[p + 1])):
                coarse.right[base // 2 + p // 2, j] = 0.5 * value

    blocks(level, body)


def restrict_sigma(level, coarse):
    def body(base, count):
        for p in range(0, count, 2):
            low = [level.sigma[base + p + 1, j] for j in range(level.rows)]
            high = [level.sigma[base + p + 2, j] for j in range(level.rows)]
            for j, value in enumerate(summed_pairs(level, low, high)):
                coarse.sigma[base // 2 + p // 2 + 1, j] = 0.125 * value

    blocks(level, body)


def correct(level, field, coarse, window=None):
    def body(base, count):
        for p in range(count):
            for j in range(level.rows):
                e = coarse.field[base // 2 + p // 2 + 1, j * coarse.rows // level.rows]
                field[base + p + 1, j] = field[base + p + 1, j] + e

    blocks(level, body, window)


def coarse_solve(levels, index):
    level = levels[index]
    if index == len(levels) - 1:
        red_from_zero(level, level.field)
        half_sweep(level, level.field, 1)
        for _ in range(COARSE_SWEEPS - 1):
            half_sweep(level, level.field, 0)
            half_sweep(level, level.field, 1)
        return
    red_from_zero(level, level.field)
    half_sweep(level, level.field, 1)
    restrict_residual(level, level.field, levels[index + 1])
    coarse_solve(levels, index + 1)
    correct(level, level.field, levels[index + 1])
    half_sweep(level, level.field, 0)
    half_sweep(level, level.field, 1)


class SigmaRows:
    def __init__(self, ref):
        self.ref = ref

    def __getitem__(self, at):
        return self.ref[at[1] // 2, at[0], at[1] % 2]

    def __setitem__(self, at, value):
        self.ref[at[1] // 2, at[0], at[1] % 2] = value


class Fine:
    def __init__(self, level, field, right, edge_x, edge_in, edge_out, edge_up, edge_down, diagonal, inverse):
        self.level, self.planes, self.unroll = level, level.planes, level.unroll
        self.field, self.right = field, right
        self.edge_x, self.edge_in, self.edge_out = edge_x, edge_in, edge_out
        self.edge_up, self.edge_down = edge_up, edge_down
        self.diagonal, self.inverse = diagonal, inverse

    def first_row(self, plane, colour):
        return self.level.even if (plane + colour) % 2 == 0 else self.level.odd

    def rows(self, field, at, plane):
        first = self.first_row(plane, 0)
        red = [field[0, at, k] for k in range(2)]
        black = [field[1, at, k] for k in range(2)]
        return [
            jnp.where(first, red[k], black[k]) if j == 0 else jnp.where(first, black[k], red[k])
            for k in range(2)
            for j in range(2)
        ]


def fine_setup(fine, sigma):
    level = fine.level

    def body(base, count):
        for p in range(count):
            mid = [sigma[base + p + 1, j] for j in range(4)]
            over = [sigma[base + p + 2, j] for j in range(4)]
            under = [sigma[base + p, j] for j in range(4)]
            edge_x = [m + o for m, o in zip(mid, over)]
            y_above = mid[1:] + [jnp.where(level.last_y, 0.0, level.y_up(mid[0]))]
            y_below = [jnp.where(level.first_y, 0.0, level.y_down(mid[3]))] + mid[:3]
            z_above = [jnp.where(level.last_z, 0.0, level.z_up(m)) for m in mid]
            z_below = [jnp.where(level.first_z, 0.0, level.z_down(m)) for m in mid]
            edge_y = [m + a for m, a in zip(mid, y_above)]
            edge_y[3] = jnp.where(level.last_y, 0.0, edge_y[3])
            edge_y_below = [level.y_down(edge_y[3])] + edge_y[:3]
            edge_up = [jnp.where(level.last_z, 0.0, m + a) for m, a in zip(mid, z_above)]
            edge_down = [jnp.where(level.first_z, 0.0, m + b) for m, b in zip(mid, z_below)]
            diagonal = [
                edge_x[j] + (mid[j] + under[j]) + (4.0 * mid[j] + ((y_above[j] + y_below[j]) + (z_above[j] + z_below[j])))
                for j in range(4)
            ]
            for k in range(2):
                fine.edge_in[base + p, k] = edge_y[2 * k]
                for colour in range(2):
                    first = fine.first_row(p, colour)

                    def packed(rows, k=k, first=first):
                        return jnp.where(first, rows[2 * k], rows[2 * k + 1])

                    total = packed(diagonal)
                    fine.edge_x[colour, base + p + 1, k] = packed(edge_x)
                    fine.edge_out[colour, base + p, k] = jnp.where(first, edge_y_below[2 * k], edge_y[2 * k + 1])
                    fine.edge_up[colour, base + p, k] = packed(edge_up)
                    fine.edge_down[colour, base + p, k] = packed(edge_down)
                    fine.diagonal[colour, base + p, k] = total
                    fine.inverse[colour, base + p, k] = 1.0 / total

    for colour in range(2):
        for k in range(2):
            fine.edge_x[colour, 0, k] = jnp.zeros((SUB, LANES), jnp.float32)
    blocks(level, body)


def fine_gathered(fine, field, colour, base, count):
    level = fine.level
    other = [[field[1 - colour, base + p, k] for k in range(2)] for p in range(count + 2)]
    sums = []
    for p in range(count):
        mid = other[p + 1]
        first = fine.first_row(p, colour)
        y_out = [
            jnp.where(first, level.y_down(mid[1]), mid[1]),
            jnp.where(first, mid[0], level.y_up(mid[0])),
        ]
        for k in range(2):
            total = fine.right[colour, base + p, k] + fine.edge_x[colour, base + p + 1, k] * other[p + 2][k]
            total = total + fine.edge_x[1 - colour, base + p, k] * other[p][k]
            total = total + fine.edge_in[base + p, k] * mid[k]
            total = total + fine.edge_out[colour, base + p, k] * y_out[k]
            z_sum = fine.edge_up[colour, base + p, k] * level.z_up(mid[k])
            z_sum = z_sum + fine.edge_down[colour, base + p, k] * level.z_down(mid[k])
            sums.append(total + z_sum)
    return sums


def fine_half_sweep(fine, field, colour, window=None):
    def body(base, count):
        for at, total in enumerate(fine_gathered(fine, field, colour, base, count)):
            p, k = at // 2, at % 2
            field[colour, base + p + 1, k] = total * fine.inverse[colour, base + p, k]

    blocks(fine.level, body, window)


def fine_red_from_zero(fine, field):
    def body(base, count):
        for p in range(count):
            for k in range(2):
                field[0, base + p + 1, k] = fine.right[0, base + p, k] * fine.inverse[0, base + p, k]

    blocks(fine.level, body)


def fine_restrict_residual(fine, field, coarse):
    level = fine.level

    def body(base, count):
        left = [0.0] * (2 * count)
        for colour in range(2):
            for at, total in enumerate(fine_gathered(fine, field, colour, base, count)):
                p, k = at // 2, at % 2
                left[at] += total - fine.diagonal[colour, base + p, k] * field[colour, base + p + 1, k]
        for p in range(0, count, 2):
            for k in range(2):
                value = left[2 * p + k] + left[2 * p + 2 + k]
                value = value + jnp.where(level.z_even, level.z_up(value), level.z_down(value))
                coarse.right[base // 2 + p // 2, k] = 0.5 * value

    blocks(level, body)


def fine_correct(fine, field, coarse, window=None):
    def body(base, count):
        for p in range(count):
            for k in range(2):
                e = coarse.field[base // 2 + p // 2 + 1, k]
                field[1, base + p + 1, k] = field[1, base + p + 1, k] + e

    blocks(fine.level, body, window)


def cell_of(flat):
    x, y, z = flat >> 12, (flat >> 7) & 31, flat & 127
    return (x + y + z) & 1, x, (y >> 1) & 1, y >> 2, z


def kernel(masks, total, ints, floats, *refs):
    parts = len(masks)
    sigma_parts, prior_parts = refs[:parts], refs[parts : 2 * parts]
    potential_out, misfit_out, low_out, high_out = refs[2 * parts : 2 * parts + 4]
    scratch = list(refs[2 * parts + 4 :])
    staged, left, forward = [scratch.pop(0) for _ in range(3)]
    local = prior_parts[0].shape[0]
    fine = Fine(Level(0, total, *[None] * 8), *[scratch.pop(0) for _ in range(9)])
    adjoint = fine.field
    sigma = SigmaRows(adjoint)
    grid = fine.level
    grid.sigma = sigma
    levels = [grid] + [Level(index, total >> index, *[scratch.pop(0) for _ in range(8)]) for index in range(1, LEVELS)]
    position = ints[0]
    receivers = ints.shape[0] - 3
    zero = jnp.zeros((SUB, LANES), jnp.float32)

    def clear_ends(field):
        for colour in range(2):
            for k in range(2):
                field[colour, 0, k] = zero
                field[colour, total + 1, k] = zero

    for level in levels[1:]:
        for ref in (level.field, level.sigma):
            for j in range(level.rows):
                ref[0, j] = zero
                ref[level.planes + 1, j] = zero
    clear_ends(forward)
    clear_ends(adjoint)

    for mask, sigma_part, prior_part in zip(masks, sigma_parts, prior_parts):
        base = (position ^ mask) * local
        for plane in range(local):
            for j in range(4):
                sigma[base + plane + 1, j] = sigma_part[plane, pl.ds(j, SUB, stride=4), :]
            for k in range(2):
                forward[1, base + plane + 1, k] = prior_part[plane, k]
                for colour in range(2):
                    fine.right[colour, base + plane, k] = zero

    fine_setup(fine, sigma)
    for index in range(LEVELS - 1):
        restrict_sigma(levels[index], levels[index + 1])
        setup(levels[index + 1])
    clear_ends(adjoint)

    lane = lax.broadcasted_iota(jnp.int32, (1, LANES), 1)
    for which, sign in ((0, 2.0), (1, -2.0)):
        colour, x, k, s, z = cell_of(ints[1 + which])
        row = fine.right[colour, x, k, pl.ds(s, 1), :]
        fine.right[colour, x, k, pl.ds(s, 1), :] = row + jnp.where(lane == z, sign * floats[0], 0.0)

    fine_half_sweep(fine, forward, 0)
    fine_half_sweep(fine, forward, 1)
    fine_restrict_residual(fine, forward, levels[1])
    coarse_solve(levels, 1)
    fine_correct(fine, forward, levels[1])
    fine_half_sweep(fine, forward, 0)
    fine_half_sweep(fine, forward, 1)

    first = position * local
    for plane in range(local):
        for j, row in enumerate(fine.rows(forward, first + plane + 1, plane)):
            staged[0, plane, pl.ds(j, SUB, stride=4), :] = row
    potential_copy = pltpu.make_async_copy(staged, potential_out, left)
    potential_copy.start()

    for which in range(2):
        colour, x, k, s, z = cell_of(ints[1 + which])
        fine.right[colour, x, k, pl.ds(s, 1), :] = jnp.zeros((1, LANES), jnp.float32)

    def receive(i, carry):
        colour, x, k, s, z = cell_of(ints[3 + i])
        value = jnp.where(lane == z, forward[colour, x + 1, k, pl.ds(s, 1), :] - floats[1 + i], 0.0)
        misfit_out[pl.ds(i, 1), :] = value
        fine.right[colour, x, k, pl.ds(s, 1), :] = fine.right[colour, x, k, pl.ds(s, 1), :] + 2.0 * value
        return carry

    lax.fori_loop(0, receivers, receive, 0, unroll=32)

    def window(margin):
        count = min(local + 2 * margin, total)
        return jnp.clip(first - margin, 0, total - count), count

    fine_red_from_zero(fine, adjoint)
    fine_half_sweep(fine, adjoint, 1)
    fine_restrict_residual(fine, adjoint, levels[1])
    coarse_solve(levels, 1)
    fine_correct(fine, adjoint, levels[1], window(4))
    fine_half_sweep(fine, adjoint, 0, window(2))
    fine_half_sweep(fine, adjoint, 1, window(2))

    def gradient(base, out):
        ahead = [[fine.rows(field, base + p, p + 1) for field in (forward, adjoint)] for p in range(2)]
        for plane in range(local // 2):
            (under_p, under_a), (p, a) = ahead
            over_p, over_a = [fine.rows(field, base + plane + 2, plane + 1) for field in (forward, adjoint)]
            ahead = [(p, a), (over_p, over_a)]
            y_pairs = []
            for j in range(4):
                if j < 3:
                    up_p, up_a = p[j + 1], a[j + 1]
                else:
                    up_p = jnp.where(grid.last_y, 0.0, grid.y_up(p[0]))
                    up_a = jnp.where(grid.last_y, 0.0, grid.y_up(a[0]))
                y_pairs.append((p[j] - up_p) * (a[j] - up_a))
            for j in range(4):
                own = p[j] * a[j]
                value = (p[j] - under_p[j]) * (a[j] - under_a[j])
                value = value + (p[j] - over_p[j]) * (a[j] - over_a[j])
                if j > 0:
                    y_below = y_pairs[j - 1]
                else:
                    y_below = jnp.where(grid.first_y, own, grid.y_down(y_pairs[3]))
                value = value + (y_pairs[j] + y_below)
                up_p = jnp.where(grid.last_z, 0.0, grid.z_up(p[j]))
                up_a = jnp.where(grid.last_z, 0.0, grid.z_up(a[j]))
                z_pair = (p[j] - up_p) * (a[j] - up_a)
                z_below = jnp.where(grid.first_z, own, grid.z_down(z_pair))
                value = value + (z_pair + z_below)
                out[plane, pl.ds(j, SUB, stride=4), :] = -0.5 * value

    gradient(first, low_out)
    gradient(first + local // 2, high_out)
    potential_copy.wait()


def black_kernel(prior, out):
    fine = Fine(Level(0, prior.shape[1], *[None] * 8), *[None] * 9)
    for plane in range(prior.shape[1]):
        first = fine.first_row(plane, 1)
        rows = [prior[0, plane, pl.ds(j, SUB, stride=4), :] for j in range(4)]
        for k in range(2):
            out[plane, k] = jnp.where(first, rows[2 * k], rows[2 * k + 1])


def black_cells(prior):
    return pl.pallas_call(
        black_kernel,
        out_shape=jax.ShapeDtypeStruct((prior.shape[1], 2, SUB, LANES), jnp.float32),
        name="black_cells",
    )(prior)


def solve(sigma_parts, prior_parts, masks, ints, floats):
    local, cells_y, cells_z = sigma_parts[0].shape
    parts = len(masks)
    total = local * parts
    receivers = floats.shape[0] - 1

    def planes(count, index):
        return pltpu.VMEM((count, ROWS[index], SUB, LANES), jnp.float32)

    def packed(count):
        return pltpu.VMEM((2, count, 2, SUB, LANES), jnp.float32)

    slab = (local, cells_y, cells_z)
    scratch = [pltpu.VMEM((1, *slab), jnp.float32), pltpu.SemaphoreType.DMA, packed(total + 2)]
    scratch += [packed(total + 2), packed(total), packed(total + 1)]
    scratch += [pltpu.VMEM((total, 2, SUB, LANES), jnp.float32)] + [packed(total) for _ in range(5)]
    for index in range(1, LEVELS):
        n = total >> index
        scratch += [planes(n + 2, index), planes(n, index), planes(n + 1, index)]
        scratch += [planes(n, index) for _ in range(4)] + [planes(n + 2, index)]
    held = 4 * sum(math.prod(s.shape) for s in scratch[2:])
    held += 4 * cells_y * cells_z * local * (2 * parts + 3) + 4 * LANES * receivers
    half = jax.ShapeDtypeStruct((local // 2, cells_y, cells_z), jnp.float32)
    smem = pl.BlockSpec(memory_space=pltpu.SMEM)
    vmem = pl.BlockSpec(memory_space=pltpu.VMEM)
    hbm = pl.BlockSpec(memory_space=pl.ANY)
    return pl.pallas_call(
        functools.partial(kernel, masks, total),
        out_shape=(
            jax.ShapeDtypeStruct((1, local, cells_y, cells_z), jnp.float32),
            jax.ShapeDtypeStruct((receivers, LANES), jnp.float32),
            half,
            half,
        ),
        in_specs=[smem] * 2 + [vmem] * (2 * parts),
        out_specs=[hbm] + [vmem] * 3,
        scratch_shapes=scratch,
        compiler_params=pltpu.CompilerParams(vmem_limit_bytes=min(held + (6 << 20), 63 << 20)),
        name="both_cycles",
    )(ints, floats, *sigma_parts, *prior_parts)


def exchanged(value, axis, mask):
    return lax.ppermute(value, axis, [(i, i ^ mask) for i in range(lax.axis_size(axis))])


def body(conductivity, prior_potential, electrodes, currents, receivers, observed):
    count = lax.axis_size("space")
    position = lax.axis_index("space")
    black = black_cells(prior_potential)
    sigma_parts, prior_parts, masks = [conductivity], [black], [0]
    bit = count // 2
    while bit:
        sigma_parts += [exchanged(part, "space", bit) for part in sigma_parts]
        if bit > 1:
            prior_parts += [exchanged(part, "space", bit) for part in prior_parts]
        masks += [mask ^ bit for mask in masks]
        bit //= 2
    ints = jnp.concatenate([position[None], electrodes[0], receivers])
    floats = jnp.concatenate([currents, observed[0]])
    pair = masks.index(1)
    sigma_back = exchanged(sigma_parts[pair], "space", 1)
    prior_pair = exchanged(black, "space", 1)
    prior_back = exchanged(prior_pair, "space", 1)
    *far, sigma_back, prior_pair, prior_back, ints, floats = lax.optimization_barrier(
        (*prior_parts[1:], sigma_back, prior_pair, prior_back, ints, floats)
    )
    sigma_parts[0] = sigma_back
    prior_parts = [prior_back, *far, prior_pair] + [exchanged(part, "space", 1) for part in far]
    potential, picked, low, high = solve(
        sigma_parts, prior_parts, tuple(masks), ints, floats
    )
    misfit = jnp.sum(picked, axis=1)[None, :]
    orders = [[1], [1]]
    while orders[0][-1] < lax.axis_size("src") - 1:
        step = 2 * orders[0][-1] + 1
        orders = [orders[0] + [step], orders[1][:-1] + [step, orders[1][-1]]]
    for step_low, step_high in zip(*orders):
        from_low = exchanged(low, "src", step_low)
        from_high = exchanged(high, "src", step_high)
        low, high = low + from_low, high + from_high
    return potential, misfit, jnp.concatenate([low, high], 0)


def solution(mesh):
    return jax.shard_map(
        body,
        mesh=mesh,
        in_specs=(
            P(("group", "space"), None, None),
            P(("group", "src"), "space", None, None),
            P(("group", "src"), None),
            P(("group", "src")),
            P("group"),
            P(("group", "src"), None),
        ),
        out_specs=(
            P(("group", "src"), "space", None, None),
            P(("group", "src"), None),
            P(("group", "space"), None, None),
        ),
        check_vma=False,
    )
```

```python
import functools
import math

import jax
import jax.numpy as jnp
from jax import lax
from jax.experimental import pallas as pl
from jax.experimental.pallas import tpu as pltpu
from jax.sharding import PartitionSpec as P

LEVELS = 4
COARSE_SWEEPS = 4
SUB = 8
LANES = 128
ROWS = (4, 2, 1, 1)
Y_STEP = (1, 1, 1, 2)
UNROLL = (32, 32, 16, 8)


class Level:
    def __init__(self, index, planes, field, right, couple_x, couple_y, couple_z, diagonal, inverse, sigma):
        self.index, self.planes = index, planes
        self.rows, self.y_step, self.z_step = ROWS[index], Y_STEP[index], 1 << index
        self.field, self.right = field, right
        self.couple_x, self.couple_y, self.couple_z = couple_x, couple_y, couple_z
        self.diagonal, self.inverse, self.sigma = diagonal, inverse, sigma
        self.unroll = min(UNROLL[index], planes)
        lane = lax.broadcasted_iota(jnp.int32, (SUB, LANES), 1)
        sub = lax.broadcasted_iota(jnp.int32, (SUB, LANES), 0)
        self.lane, self.sub = lane, sub
        parity = (lane >> index) & 1
        if index == 2:
            parity = (parity + sub) & 1
        if index == 3:
            parity = (parity + (sub >> 1)) & 1
        self.even = parity == 0
        self.odd = parity == 1
        self.z_even = ((lane >> index) & 1) == 0
        self.last_z = lane >= LANES - self.z_step
        self.last_y = sub >= SUB - self.y_step
        self.first_z = lane < self.z_step
        self.first_y = sub < self.y_step

    def mask(self, plane, row, colour):
        return self.even if (plane + row + colour) % 2 == 0 else self.odd

    def z_up(self, value):
        return pltpu.roll(value, LANES - self.z_step, 1)

    def z_down(self, value):
        return pltpu.roll(value, self.z_step, 1)

    def y_up(self, value):
        return pltpu.roll(value, SUB - self.y_step, 0)

    def y_down(self, value):
        return pltpu.roll(value, self.y_step, 0)


def blocks(level, body, window=None):
    if window is not None:
        body(*window)
        return
    count = level.planes // level.unroll
    if count == 1:
        body(0, level.unroll)
        return

    def step(block, carry):
        body(block * level.unroll, level.unroll)
        return carry

    lax.fori_loop(0, count, step, 0)


def setup(level):
    rows = level.rows

    def body(base, count):
        sig = [[level.sigma[base + p, j] for j in range(rows)] for p in range(count + 2)]
        for p in range(count):
            for j in range(rows):
                mid = sig[p + 1][j]
                above = mid + sig[p + 2][j]
                below = mid + sig[p][j]
                if j + 1 < rows:
                    y_above = sig[p + 1][j + 1]
                else:
                    y_above = jnp.where(level.last_y, 0.0, level.y_up(sig[p + 1][0]))
                if j > 0:
                    y_below = sig[p + 1][j - 1]
                else:
                    y_below = jnp.where(level.first_y, 0.0, level.y_down(sig[p + 1][rows - 1]))
                z_above = jnp.where(level.last_z, 0.0, level.z_up(mid))
                z_below = jnp.where(level.first_z, 0.0, level.z_down(mid))
                diagonal = above + below + (4.0 * mid + ((y_above + y_below) + (z_above + z_below)))
                level.couple_x[base + p + 1, j] = above
                if j + 1 < rows:
                    level.couple_y[base + p, j] = mid + y_above
                else:
                    level.couple_y[base + p, j] = jnp.where(level.last_y, 0.0, mid + y_above)
                level.couple_z[base + p, j] = jnp.where(level.last_z, 0.0, mid + z_above)
                level.diagonal[base + p, j] = diagonal
                level.inverse[base + p, j] = 1.0 / diagonal

    for j in range(rows):
        level.couple_x[0, j] = jnp.zeros((SUB, LANES), jnp.float32)
    blocks(level, body)


def gathered(level, field, base, count):
    rows = level.rows
    planes = [[field[base + p, j] for j in range(rows)] for p in range(count + 2)]
    couple_x = [[level.couple_x[base + p, j] for j in range(rows)] for p in range(count + 1)]
    sums = []
    for p in range(count):
        mid = planes[p + 1]
        couple_y = [level.couple_y[base + p, j] for j in range(rows)]
        row = []
        for j in range(rows):
            couple_z = level.couple_z[base + p, j]
            total = level.right[base + p, j] + couple_x[p + 1][j] * planes[p + 2][j]
            total = total + couple_x[p][j] * planes[p][j]
            y_above = mid[j + 1] if j + 1 < rows else level.y_up(mid[0])
            total = total + couple_y[j] * y_above
            if j > 0:
                total = total + couple_y[j - 1] * mid[j - 1]
            else:
                total = total + level.y_down(couple_y[rows - 1] * mid[rows - 1])
            total = total + (couple_z * level.z_up(mid[j]) + level.z_down(couple_z * mid[j]))
            row.append(total)
        sums.append(row)
    return sums, planes


def half_sweep(level, field, colour, window=None):
    def body(base, count):
        sums, planes = gathered(level, field, base, count)
        for p in range(count):
            for j in range(level.rows):
                update = sums[p][j] * level.inverse[base + p, j]
                field[base + p + 1, j] = jnp.where(level.mask(p, j, colour), update, planes[p + 1][j])

    blocks(level, body, window)


def red_from_zero(level, field):
    def body(base, count):
        for p in range(count):
            for j in range(level.rows):
                update = level.right[base + p, j] * level.inverse[base + p, j]
                field[base + p + 1, j] = jnp.where(level.mask(p, j, 0), update, 0.0)

    blocks(level, body)


def summed_pairs(level, low, high):
    both = [a + b for a, b in zip(low, high)]
    if level.rows > 1:
        both = [both[j] + both[j + 1] for j in range(0, level.rows, 2)]
    else:
        both = [v + jnp.where((level.sub & 1) == 0, level.y_up(v), level.y_down(v)) for v in both]
    return [v + jnp.where(level.z_even, level.z_up(v), level.z_down(v)) for v in both]


def restrict_residual(level, field, coarse):
    def body(base, count):
        sums, planes = gathered(level, field, base, count)
        left = [
            [sums[p][j] - level.diagonal[base + p, j] * planes[p + 1][j] for j in range(level.rows)]
            for p in range(count)
        ]
        for p in range(0, count, 2):
            for j, value in enumerate(summed_pairs(level, left[p], left[p + 1])):
                coarse.right[base // 2 + p // 2, j] = 0.5 * value

    blocks(level, body)


def restrict_sigma(level, coarse):
    def body(base, count):
        for p in range(0, count, 2):
            low = [level.sigma[base + p + 1, j] for j in range(level.rows)]
            high = [level.sigma[base + p + 2, j] for j in range(level.rows)]
            for j, value in enumerate(summed_pairs(level, low, high)):
                coarse.sigma[base // 2 + p // 2 + 1, j] = 0.125 * value

    blocks(level, body)


def correct(level, field, coarse, window=None):
    def body(base, count):
        for p in range(count):
            for j in range(level.rows):
                e = coarse.field[base // 2 + p // 2 + 1, j * coarse.rows // level.rows]
                field[base + p + 1, j] = field[base + p + 1, j] + e

    blocks(level, body, window)


def coarse_solve(levels, index):
    level = levels[index]
    if index == len(levels) - 1:
        red_from_zero(level, level.field)
        half_sweep(level, level.field, 1)
        for _ in range(COARSE_SWEEPS - 1):
            half_sweep(level, level.field, 0)
            half_sweep(level, level.field, 1)
        return
    red_from_zero(level, level.field)
    half_sweep(level, level.field, 1)
    restrict_residual(level, level.field, levels[index + 1])
    coarse_solve(levels, index + 1)
    correct(level, level.field, levels[index + 1])
    half_sweep(level, level.field, 0)
    half_sweep(level, level.field, 1)


class SigmaRows:
    def __init__(self, ref):
        self.ref = ref

    def __getitem__(self, at):
        return self.ref[at[1] // 2, at[0], at[1] % 2]

    def __setitem__(self, at, value):
        self.ref[at[1] // 2, at[0], at[1] % 2] = value


class Fine:
    def __init__(self, level, field, right, edge_x, edge_in, edge_out, edge_up, edge_down, diagonal, inverse):
        self.level, self.planes, self.unroll = level, level.planes, level.unroll
        self.field, self.right = field, right
        self.edge_x, self.edge_in, self.edge_out = edge_x, edge_in, edge_out
        self.edge_up, self.edge_down = edge_up, edge_down
        self.diagonal, self.inverse = diagonal, inverse

    def first_row(self, plane, colour):
        return self.level.even if (plane + colour) % 2 == 0 else self.level.odd

    def rows(self, field, at, plane):
        first = self.first_row(plane, 0)
        red = [field[0, at, k] for k in range(2)]
        black = [field[1, at, k] for k in range(2)]
        return [
            jnp.where(first, red[k], black[k]) if j == 0 else jnp.where(first, black[k], red[k])
            for k in range(2)
            for j in range(2)
        ]


def fine_setup(fine, sigma):
    level = fine.level

    def body(base, count):
        for p in range(count):
            mid = [sigma[base + p + 1, j] for j in range(4)]
            over = [sigma[base + p + 2, j] for j in range(4)]
            under = [sigma[base + p, j] for j in range(4)]
            edge_x = [m + o for m, o in zip(mid, over)]
            y_above = mid[1:] + [jnp.where(level.last_y, 0.0, level.y_up(mid[0]))]
            y_below = [jnp.where(level.first_y, 0.0, level.y_down(mid[3]))] + mid[:3]
            z_above = [jnp.where(level.last_z, 0.0, level.z_up(m)) for m in mid]
            z_below = [jnp.where(level.first_z, 0.0, level.z_down(m)) for m in mid]
            edge_y = [m + a for m, a in zip(mid, y_above)]
            edge_y[3] = jnp.where(level.last_y, 0.0, edge_y[3])
            edge_y_below = [level.y_down(edge_y[3])] + edge_y[:3]
            edge_up = [jnp.where(level.last_z, 0.0, m + a) for m, a in zip(mid, z_above)]
            edge_down = [jnp.where(level.first_z, 0.0, m + b) for m, b in zip(mid, z_below)]
            diagonal = [
                edge_x[j] + (mid[j] + under[j]) + (4.0 * mid[j] + ((y_above[j] + y_below[j]) + (z_above[j] + z_below[j])))
                for j in range(4)
            ]
            for k in range(2):
                fine.edge_in[base + p, k] = edge_y[2 * k]
                for colour in range(2):
                    first = fine.first_row(p, colour)

                    def packed(rows, k=k, first=first):
                        return jnp.where(first, rows[2 * k], rows[2 * k + 1])

                    total = packed(diagonal)
                    fine.edge_x[colour, base + p + 1, k] = packed(edge_x)
                    fine.edge_out[colour, base + p, k] = jnp.where(first, edge_y_below[2 * k], edge_y[2 * k + 1])
                    fine.edge_up[colour, base + p, k] = packed(edge_up)
                    fine.edge_down[colour, base + p, k] = packed(edge_down)
                    fine.diagonal[colour, base + p, k] = total
                    fine.inverse[colour, base + p, k] = 1.0 / total

    for colour in range(2):
        for k in range(2):
            fine.edge_x[colour, 0, k] = jnp.zeros((SUB, LANES), jnp.float32)
    blocks(level, body)


def fine_gathered(fine, field, colour, base, count):
    level = fine.level
    other = [[field[1 - colour, base + p, k] for k in range(2)] for p in range(count + 2)]
    sums = []
    for p in range(count):
        mid = other[p + 1]
        first = fine.first_row(p, colour)
        y_out = [
            jnp.where(first, level.y_down(mid[1]), mid[1]),
            jnp.where(first, mid[0], level.y_up(mid[0])),
        ]
        for k in range(2):
            total = fine.right[colour, base + p, k] + fine.edge_x[colour, base + p + 1, k] * other[p + 2][k]
            total = total + fine.edge_x[1 - colour, base + p, k] * other[p][k]
            total = total + fine.edge_in[base + p, k] * mid[k]
            total = total + fine.edge_out[colour, base + p, k] * y_out[k]
            z_sum = fine.edge_up[colour, base + p, k] * level.z_up(mid[k])
            z_sum = z_sum + fine.edge_down[colour, base + p, k] * level.z_down(mid[k])
            sums.append(total + z_sum)
    return sums


def fine_half_sweep(fine, field, colour, window=None):
    def body(base, count):
        for at, total in enumerate(fine_gathered(fine, field, colour, base, count)):
            p, k = at // 2, at % 2
            field[colour, base + p + 1, k] = total * fine.inverse[colour, base + p, k]

    blocks(fine.level, body, window)


def fine_red_from_zero(fine, field):
    def body(base, count):
        for p in range(count):
            for k in range(2):
                field[0, base + p + 1, k] = fine.right[0, base + p, k] * fine.inverse[0, base + p, k]

    blocks(fine.level, body)


def fine_restrict_residual(fine, field, coarse):
    level = fine.level

    def body(base, count):
        left = [0.0] * (2 * count)
        for colour in range(2):
            for at, total in enumerate(fine_gathered(fine, field, colour, base, count)):
                p, k = at // 2, at % 2
                left[at] += total - fine.diagonal[colour, base + p, k] * field[colour, base + p + 1, k]
        for p in range(0, count, 2):
            for k in range(2):
                value = left[2 * p + k] + left[2 * p + 2 + k]
                value = value + jnp.where(level.z_even, level.z_up(value), level.z_down(value))
                coarse.right[base // 2 + p // 2, k] = 0.5 * value

    blocks(level, body)


def fine_correct(fine, field, coarse, window=None):
    def body(base, count):
        for p in range(count):
            for k in range(2):
                e = coarse.field[base // 2 + p // 2 + 1, k]
                field[1, base + p + 1, k] = field[1, base + p + 1, k] + e

    blocks(fine.level, body, window)


def cell_of(flat):
    x, y, z = flat >> 12, (flat >> 7) & 31, flat & 127
    return (x + y + z) & 1, x, (y >> 1) & 1, y >> 2, z


def kernel(masks, total, ints, floats, *refs):
    parts = len(masks)
    sigma_parts, prior_parts = refs[:parts], refs[parts : 2 * parts]
    potential_out, misfit_out, low_out, high_out = refs[2 * parts : 2 * parts + 4]
    scratch = list(refs[2 * parts + 4 :])
    staged, left, forward = [scratch.pop(0) for _ in range(3)]
    local = prior_parts[0].shape[0]
    fine = Fine(Level(0, total, *[None] * 8), *[scratch.pop(0) for _ in range(9)])
    adjoint = fine.field
    sigma = SigmaRows(adjoint)
    grid = fine.level
    grid.sigma = sigma
    levels = [grid] + [Level(index, total >> index, *[scratch.pop(0) for _ in range(8)]) for index in range(1, LEVELS)]
    position = ints[0]
    receivers = ints.shape[0] - 3
    zero = jnp.zeros((SUB, LANES), jnp.float32)

    def clear_ends(field):
        for colour in range(2):
            for k in range(2):
                field[colour, 0, k] = zero
                field[colour, total + 1, k] = zero

    for level in levels[1:]:
        for ref in (level.field, level.sigma):
            for j in range(level.rows):
                ref[0, j] = zero
                ref[level.planes + 1, j] = zero
    clear_ends(forward)
    clear_ends(adjoint)

    for mask, sigma_part, prior_part in zip(masks, sigma_parts, prior_parts):
        base = (position ^ mask) * local
        for plane in range(local):
            for j in range(4):
                sigma[base + plane + 1, j] = sigma_part[plane, pl.ds(j, SUB, stride=4), :]
            for k in range(2):
                forward[1, base + plane + 1, k] = prior_part[plane, k]
                for colour in range(2):
                    fine.right[colour, base + plane, k] = zero

    fine_setup(fine, sigma)
    for index in range(LEVELS - 1):
        restrict_sigma(levels[index], levels[index + 1])
        setup(levels[index + 1])
    clear_ends(adjoint)

    lane = lax.broadcasted_iota(jnp.int32, (1, LANES), 1)
    for which, sign in ((0, 2.0), (1, -2.0)):
        colour, x, k, s, z = cell_of(ints[1 + which])
        row = fine.right[colour, x, k, pl.ds(s, 1), :]
        fine.right[colour, x, k, pl.ds(s, 1), :] = row + jnp.where(lane == z, sign * floats[0], 0.0)

    fine_half_sweep(fine, forward, 0)
    fine_half_sweep(fine, forward, 1)
    fine_restrict_residual(fine, forward, levels[1])
    coarse_solve(levels, 1)
    fine_correct(fine, forward, levels[1])
    fine_half_sweep(fine, forward, 0)
    fine_half_sweep(fine, forward, 1)

    first = position * local
    for plane in range(local):
        for j, row in enumerate(fine.rows(forward, first + plane + 1, plane)):
            staged[0, plane, pl.ds(j, SUB, stride=4), :] = row
    potential_copy = pltpu.make_async_copy(staged, potential_out, left)
    potential_copy.start()

    for which in range(2):
        colour, x, k, s, z = cell_of(ints[1 + which])
        fine.right[colour, x, k, pl.ds(s, 1), :] = jnp.zeros((1, LANES), jnp.float32)

    def receive(i, carry):
        colour, x, k, s, z = cell_of(ints[3 + i])
        value = jnp.where(lane == z, forward[colour, x + 1, k, pl.ds(s, 1), :] - floats[1 + i], 0.0)
        misfit_out[pl.ds(i, 1), :] = value
        fine.right[colour, x, k, pl.ds(s, 1), :] = fine.right[colour, x, k, pl.ds(s, 1), :] + 2.0 * value
        return carry

    lax.fori_loop(0, receivers, receive, 0, unroll=32)

    def window(margin):
        count = min(local + 2 * margin, total)
        return jnp.clip(first - margin, 0, total - count), count

    fine_red_from_zero(fine, adjoint)
    fine_half_sweep(fine, adjoint, 1)
    fine_restrict_residual(fine, adjoint, levels[1])
    coarse_solve(levels, 1)
    fine_correct(fine, adjoint, levels[1], window(4))
    fine_half_sweep(fine, adjoint, 0, window(2))
    fine_half_sweep(fine, adjoint, 1, window(2))

    def gradient(base, out, count):
        ahead = [[fine.rows(field, base + p, p + 1) for field in (forward, adjoint)] for p in range(2)]
        for plane in range(count):
            (under_p, under_a), (p, a) = ahead
            over_p, over_a = [fine.rows(field, base + plane + 2, plane + 1) for field in (forward, adjoint)]
            ahead = [(p, a), (over_p, over_a)]
            y_pairs = []
            for j in range(4):
                if j < 3:
                    up_p, up_a = p[j + 1], a[j + 1]
                else:
                    up_p = jnp.where(grid.last_y, 0.0, grid.y_up(p[0]))
                    up_a = jnp.where(grid.last_y, 0.0, grid.y_up(a[0]))
                y_pairs.append((p[j] - up_p) * (a[j] - up_a))
            for j in range(4):
                own = p[j] * a[j]
                value = (p[j] - under_p[j]) * (a[j] - under_a[j])
                value = value + (p[j] - over_p[j]) * (a[j] - over_a[j])
                if j > 0:
                    y_below = y_pairs[j - 1]
                else:
                    y_below = jnp.where(grid.first_y, own, grid.y_down(y_pairs[3]))
                value = value + (y_pairs[j] + y_below)
                up_p = jnp.where(grid.last_z, 0.0, grid.z_up(p[j]))
                up_a = jnp.where(grid.last_z, 0.0, grid.z_up(a[j]))
                z_pair = (p[j] - up_p) * (a[j] - up_a)
                z_below = jnp.where(grid.first_z, own, grid.z_down(z_pair))
                value = value + (z_pair + z_below)
                out[plane, pl.ds(j, SUB, stride=4), :] = -0.5 * value

    low_planes = low_out.shape[0]
    gradient(first, low_out, low_planes)
    gradient(first + low_planes, high_out, local - low_planes)
    potential_copy.wait()


def black_kernel(prior, out):
    fine = Fine(Level(0, prior.shape[1], *[None] * 8), *[None] * 9)
    for plane in range(prior.shape[1]):
        first = fine.first_row(plane, 1)
        rows = [prior[0, plane, pl.ds(j, SUB, stride=4), :] for j in range(4)]
        for k in range(2):
            out[plane, k] = jnp.where(first, rows[2 * k], rows[2 * k + 1])


def black_cells(prior):
    return pl.pallas_call(
        black_kernel,
        out_shape=jax.ShapeDtypeStruct((prior.shape[1], 2, SUB, LANES), jnp.float32),
        name="black_cells",
    )(prior)


def solve(sigma_parts, prior_parts, masks, ints, floats):
    local, cells_y, cells_z = sigma_parts[0].shape
    parts = len(masks)
    total = local * parts
    receivers = floats.shape[0] - 1

    def planes(count, index):
        return pltpu.VMEM((count, ROWS[index], SUB, LANES), jnp.float32)

    def packed(count):
        return pltpu.VMEM((2, count, 2, SUB, LANES), jnp.float32)

    slab = (local, cells_y, cells_z)
    scratch = [pltpu.VMEM((1, *slab), jnp.float32), pltpu.SemaphoreType.DMA, packed(total + 2)]
    scratch += [packed(total + 2), packed(total), packed(total + 1)]
    scratch += [pltpu.VMEM((total, 2, SUB, LANES), jnp.float32)] + [packed(total) for _ in range(5)]
    for index in range(1, LEVELS):
        n = total >> index
        scratch += [planes(n + 2, index), planes(n, index), planes(n + 1, index)]
        scratch += [planes(n, index) for _ in range(4)] + [planes(n + 2, index)]
    held = 4 * sum(math.prod(s.shape) for s in scratch[2:])
    held += 4 * cells_y * cells_z * local * (2 * parts + 3) + 4 * LANES * receivers
    low_planes = 2 * (local * 5 // 16)
    low, high = [jax.ShapeDtypeStruct((n, cells_y, cells_z), jnp.float32) for n in (low_planes, local - low_planes)]
    smem = pl.BlockSpec(memory_space=pltpu.SMEM)
    vmem = pl.BlockSpec(memory_space=pltpu.VMEM)
    hbm = pl.BlockSpec(memory_space=pl.ANY)
    return pl.pallas_call(
        functools.partial(kernel, masks, total),
        out_shape=(
            jax.ShapeDtypeStruct((1, local, cells_y, cells_z), jnp.float32),
            jax.ShapeDtypeStruct((receivers, LANES), jnp.float32),
            low,
            high,
        ),
        in_specs=[smem] * 2 + [vmem] * (2 * parts),
        out_specs=[hbm] + [vmem] * 3,
        scratch_shapes=scratch,
        compiler_params=pltpu.CompilerParams(vmem_limit_bytes=min(held + (6 << 20), 63 << 20)),
        name="both_cycles",
    )(ints, floats, *sigma_parts, *prior_parts)


def exchanged(value, axis, mask):
    return lax.ppermute(value, axis, [(i, i ^ mask) for i in range(lax.axis_size(axis))])


def body(conductivity, prior_potential, electrodes, currents, receivers, observed):
    count = lax.axis_size("space")
    position = lax.axis_index("space")
    black = black_cells(prior_potential)
    sigma_parts, prior_parts, masks = [conductivity], [black], [0]
    bit = count // 2
    while bit:
        sigma_parts += [exchanged(part, "space", bit) for part in sigma_parts]
        if bit > 1:
            prior_parts += [exchanged(part, "space", bit) for part in prior_parts]
        masks += [mask ^ bit for mask in masks]
        bit //= 2
    ints = jnp.concatenate([position[None], electrodes[0], receivers])
    floats = jnp.concatenate([currents, observed[0]])
    pair = masks.index(1)
    sigma_back = exchanged(sigma_parts[pair], "space", 1)
    prior_pair = exchanged(black, "space", 1)
    prior_back = exchanged(prior_pair, "space", 1)
    *far, sigma_back, prior_pair, prior_back, ints, floats = lax.optimization_barrier(
        (*prior_parts[1:], sigma_back, prior_pair, prior_back, ints, floats)
    )
    sigma_parts[0] = sigma_back
    prior_parts = [prior_back, *far, prior_pair] + [exchanged(part, "space", 1) for part in far]
    potential, picked, low, high = solve(
        sigma_parts, prior_parts, tuple(masks), ints, floats
    )
    misfit = jnp.sum(picked, axis=1)[None, :]
    orders = [[1], [1]]
    while orders[0][-1] < lax.axis_size("src") - 1:
        step = 2 * orders[0][-1] + 1
        orders = [orders[0] + [step], orders[1][:-1] + [step, orders[1][-1]]]
    for step_low, step_high in zip(*orders):
        from_low = exchanged(low, "src", step_low)
        from_high = exchanged(high, "src", step_high)
        low, high = low + from_low, high + from_high
    return potential, misfit, jnp.concatenate([low, high], 0)


def solution(mesh):
    return jax.shard_map(
        body,
        mesh=mesh,
        in_specs=(
            P(("group", "space"), None, None),
            P(("group", "src"), "space", None, None),
            P(("group", "src"), None),
            P(("group", "src")),
            P("group"),
            P(("group", "src"), None),
        ),
        out_specs=(
            P(("group", "src"), "space", None, None),
            P(("group", "src"), None),
            P(("group", "space"), None, None),
        ),
        check_vma=False,
    )
```
